512 devices in a mesh: dp: 128 (over z, y, core), mp: 4 (over x).
Axes of the slice: x: 4, y: 4, z: 16, core: 2. Of those that a mesh axis runs over, the one named last changes fastest.
Arguments:
- frames_in: bfloat16 [131072, 1536], P('dp', 'mp')
- lengths: int32 [512], P('dp'), may hold values from 42 to 256, as said below
- ln_gain: float32 [1536], P('mp'), may hold values from 0.1 to 1.9
- ln_bias: float32 [1536], P('mp'), may hold values from -3 to 3
- kernel: float32 [31, 1536], P(None, 'mp'), may hold values from -1 to 1
- point_weight: bfloat16 [1536, 1536], P('dp', 'mp'), may hold values from -0.15625 to 0.15625
- target: bfloat16 [131072, 1536], P('dp')
Outputs:
- frames_grad: bfloat16 [131072, 1536], P('dp', 'mp')
- weight_grad: float32 [1536, 1536], P('dp', 'mp')
- kernel_grad: float32 [31, 1536], P(None, 'mp')
- gain_grad: float32 [1536], P('mp')
- bias_grad: float32 [1536], P('mp')
The draws below stay inside these ranges and needn't reach their ends.
Inputs may be any that keep to these rules, and one draw needn't show every extreme that they name: `lengths`: valid frames of each utterance slot; some slot has exactly 256.
All inputs are finite; a program needn't handle non-finite values.
Results may differ from the reference program's by a relative error of at most 0.001.
Values may be sent and summed in bfloat16 or wider, within the bound.
No kernel may reach another device: no remote copies, remote signals or barrier semaphores. Data moves between devices by JAX's collectives and lax.ppermute only.
A program may use at most 64 MiB of HBM per device.

```python
import math
import jax
import jax.numpy as jnp
from jax import lax

D = 1536
KERNEL = 31
UTT = 4
FRAMES = 256
TOK_DEV = 1024
TOKENS = 131072
UTTS = 512
N_DP = 128


def draw_lengths(key, part):
    slot_index = jnp.arange(UTTS, dtype=jnp.int32)
    device_index = slot_index // UTT
    floor_top = FRAMES // 3
    ceiling = floor_top + device_index * (FRAMES - floor_top) // max(N_DP - 1, 1)
    low_end = ceiling // 2
    random_bits = jax.random.randint(key, (UTTS,), 0, 1 << 20)
    drawn = low_end + random_bits % (ceiling - low_end + 1)
    drawn = jnp.where(slot_index == UTTS - 1, FRAMES, drawn)
    drawn = jnp.where(slot_index == 0, floor_top // 2, drawn)
    return drawn.astype(jnp.int32)


def draw_frames_in(key, part):
    first, second, third, fourth = jax.random.split(jax.random.fold_in(key, 11), 4)
    ramp = jnp.arange(D, dtype=jnp.float32) / max(D - 1, 1)
    col_scale = jnp.exp(jax.random.uniform(first, (D,), jnp.float32, 0.0, math.log(10.0)) + math.log(3.0) * ramp)
    offset = 0.8 * jax.random.normal(second, (D,), jnp.float32)
    row_scale = jnp.exp(jax.random.uniform(fourth, (TOKENS, 1), jnp.float32, 0.0, math.log(10.0)))
    noise = jax.random.normal(third, (TOKENS, D), jnp.float32)
    return ((offset + noise) * col_scale * row_scale).astype(jnp.bfloat16)


def draw_target(key, part):
    first, second = jax.random.split(jax.random.fold_in(key, 23), 2)
    common = jax.random.normal(first, (D,), jnp.float32)
    noise = jax.random.normal(second, (TOKENS, D), jnp.float32)
    return jnp.clip(common + noise, -6.0, 6.0).astype(jnp.bfloat16)


def level_of(stream_key, dims, shards, smallest, high):
    factor_of, own = 1.0, jax.random.fold_in(stream_key, 6)
    for axis_at, parts in shards:
        draws = jnp.exp(jax.random.uniform(jax.random.fold_in(own, axis_at), (parts,), jnp.float32, smallest / len(shards), high / len(shards)))
        factor_of = factor_of * jnp.repeat(draws, dims[axis_at] // parts).reshape([-1 if axis == axis_at else 1 for axis in range(len(dims))])
    return factor_of


def scatter_about(own_key, dims, scale, reach, shards=(), held_as=jnp.bfloat16):
    values = scale * jax.random.normal(own_key, dims, jnp.float32)
    if shards:
        values = values * level_of(own_key, dims, shards, -0.22, 0.18)
    return jnp.clip(values, -reach, reach).astype(held_as)


def setup_inputs(seed: int = 0) -> dict:
    key_of = jax.random.split(jax.random.key(seed), 8)
    frames_in = draw_frames_in(jax.random.fold_in(key_of[7], 71), 0)
    lengths = draw_lengths(jax.random.fold_in(key_of[7], 71), 0)
    ln_gain = jnp.clip(1.0 + 0.18 * jax.random.normal(key_of[2], (D,), jnp.float32), 0.1, 1.9)
    ln_bias = scatter_about(key_of[3], (D,), 0.5, 3.0, ((0, 4),), jnp.float32)
    kernel = scatter_about(key_of[4], (KERNEL, D), KERNEL ** -0.5, 1.0, ((1, 4),), jnp.float32)
    point_weight = scatter_about(key_of[5], (D, D), D ** -0.5, 0.15625, ((0, 128), (1, 4)))
    target = draw_target(jax.random.fold_in(key_of[7], 71), 0)
    return dict(frames_in=frames_in, lengths=lengths, ln_gain=ln_gain, ln_bias=ln_bias, kernel=kernel, point_weight=point_weight, target=target)


epsilon = 1e-05

def reference(frames_in, lengths, ln_gain, ln_bias, kernel, point_weight, target):
    frame_total = jnp.sum(lengths).astype(jnp.float32)
    inverse = 1.0 / frame_total
    half = (KERNEL - 1) // 2

    def block(state_carry, block_inputs):
        grad_acc, kernel_acc, gain_acc, bias_acc = state_carry
        x_block, len_block, target_block = block_inputs
        position = lax.broadcasted_iota(jnp.int32, (UTT, FRAMES), 1)
        valid_mask = (position < len_block[:, None]).astype(jnp.float32).reshape(TOK_DEV, 1)
        values = x_block.astype(jnp.float32)
        row_mean = lax.optimization_barrier(jnp.mean(values, axis=1, keepdims=True))
        centered = values - row_mean
        row_var = lax.optimization_barrier(jnp.mean(centered * centered, axis=1, keepdims=True))
        inv_std = lax.rsqrt(row_var + epsilon)
        normed = centered * inv_std
        masked = (normed * ln_gain + ln_bias) * valid_mask
        padded = jnp.pad(masked.reshape(UTT, FRAMES, D), ((0, 0), (half, half), (0, 0)))
        conv_out = jnp.zeros((UTT, FRAMES, D), jnp.float32)
        for k in range(KERNEL):
            conv_out = conv_out + kernel[k] * padded[:, k:k + FRAMES, :]
        pre_act = conv_out.reshape(TOK_DEV, D)
        gate_sig = jax.nn.sigmoid(pre_act)
        activation = (pre_act * gate_sig).astype(jnp.bfloat16)
        cotangent = target_block * valid_mask.astype(jnp.bfloat16)
        grad_acc = grad_acc + lax.dot_general(cotangent, activation, (((0,), (0,)), ((), ())), preferred_element_type=jnp.float32)
        act_grad = jnp.dot(cotangent, point_weight, preferred_element_type=jnp.float32)
        pre_grad = act_grad * gate_sig * (1.0 + pre_act * (1.0 - gate_sig))
        grad_block = pre_grad.reshape(UTT, FRAMES, D)
        grad_padded = jnp.pad(grad_block, ((0, 0), (half, half), (0, 0)))
        back_in = jnp.zeros((UTT, FRAMES, D), jnp.float32)
        kernel_rows = []
        for k in range(KERNEL):
            back_in = back_in + kernel[k] * grad_padded[:, 2 * half - k:2 * half - k + FRAMES, :]
            kernel_rows.append(lax.optimization_barrier(jnp.sum(grad_block * padded[:, k:k + FRAMES, :], axis=(0, 1))))
        kernel_part = jnp.stack(kernel_rows, axis=0)
        masked_grad = back_in.reshape(TOK_DEV, D) * valid_mask
        gain_acc = gain_acc + lax.optimization_barrier(jnp.sum(masked_grad * normed, axis=0))
        bias_acc = bias_acc + lax.optimization_barrier(jnp.sum(masked_grad, axis=0))
        kernel_acc = kernel_acc + kernel_part
        hat_grad = masked_grad * ln_gain
        norm_grad = inv_std * (hat_grad - lax.optimization_barrier(jnp.mean(hat_grad, axis=1, keepdims=True)) - normed * lax.optimization_barrier(jnp.mean(hat_grad * normed, axis=1, keepdims=True)))
        frames_out = ((cotangent.astype(jnp.float32) + norm_grad) * (TOKENS * inverse)).astype(jnp.bfloat16)
        return ((grad_acc, kernel_acc, gain_acc, bias_acc), frames_out)
    start_state = (jnp.zeros((D, D), jnp.float32), jnp.zeros((KERNEL, D), jnp.float32), jnp.zeros((D,), jnp.float32), jnp.zeros((D,), jnp.float32))
    final_state, frames_blocks = lax.scan(block, start_state, (frames_in.reshape(N_DP, TOK_DEV, D), lengths.reshape(N_DP, UTT), target.reshape(N_DP, TOK_DEV, D)))
    grad_acc, kernel_acc, gain_acc, bias_acc = final_state
    return (frames_blocks.reshape(TOKENS, D), grad_acc * inverse, kernel_acc * inverse, gain_acc * inverse, bias_acc * inverse)
```

```python
import functools

import jax
import jax.numpy as jnp
from jax import lax
from jax.experimental import pallas as pl
from jax.experimental.pallas import tpu as pltpu
from jax.sharding import Mesh, PartitionSpec as P

epsilon = 1e-05
UTT = 4
FR = 256
TOK = UTT * FR
CH = 384
LB = CH // 128
TAPS = 31
WIDTH = 1536
PADDED = FR + 32
ROWS = 32
f32 = jnp.float32
bf16 = jnp.bfloat16

VMEM = pl.BlockSpec(memory_space=pltpu.VMEM)
SMEM = pl.BlockSpec(memory_space=pltpu.SMEM)


def rows_of(column):
    return jnp.sum(column.T, axis=0, keepdims=True)


def columns_of(row):
    return jnp.broadcast_to(row, (128, FR)).T


def stats_kernel(own_ref, x_ref, out_ref):
    for u in range(UTT):
        rows = pl.ds(u * FR, FR)
        parts = [x_ref[rows, pl.ds(l * 128, 128)].astype(f32) for l in range(LB)]
        total = rows_of(parts[0] + parts[1] + parts[2])
        mean = columns_of(total * (1.0 / CH))
        parts = [p - mean for p in parts]
        square = rows_of(parts[0] * parts[0] + parts[1] * parts[1] + parts[2] * parts[2])
        for j in range(4):
            out_ref[2 * j : 2 * j + 1, rows] = jnp.where(own_ref[0] == j, total, 0.0)
            out_ref[2 * j + 1 : 2 * j + 2, rows] = jnp.where(own_ref[0] == j, square, 0.0)


def pack_kernel(part_ref, out_ref, rows_ref):
    nz, share = part_ref.shape[0], WIDTH // 128
    count = jnp.zeros((1, 128), f32)
    for z in range(nz):
        part = part_ref[z].astype(f32)
        rows_ref[z * share : (z + 1) * share, :] = part[:share]
        count = count + part[share : share + 1, :128]
    total = jnp.sum(count, axis=1, keepdims=True)
    high = jnp.floor(total * (1.0 / 256.0))
    spot = lax.broadcasted_iota(jnp.int32, (16, CH), 1) + CH * lax.broadcasted_iota(jnp.int32, (16, CH), 0)
    rows_ref[nz * share :, :] = jnp.where(spot == 0, high, jnp.where(spot == 1, total - high * 256.0, 0.0))
    packed = rows_ref[...].astype(bf16)
    for j in range(out_ref.shape[0]):
        out_ref[j] = packed


def mix_kernel(term_ref, small_ref, out_ref):
    nz, share = out_ref.shape[0], WIDTH // 128
    small = small_ref[0]
    for j in range(1, small_ref.shape[0]):
        small = small + small_ref[j]
    for z in range(nz):
        rows = term_ref[0, z * share : (z + 1) * share, :]
        for j in range(1, term_ref.shape[0]):
            rows = rows + term_ref[j, z * share : (z + 1) * share, :]
        for l in range(LB):
            out_ref[z, l * share : (l + 1) * share, :] = rows[:, l * 128 : (l + 1) * 128]
        out_ref[z, LB * share : LB * share + 16, :] = small
        out_ref[z, LB * share + 16 :, :] = jnp.zeros((4, 128), f32)


def unmix_kernel(inverse_ref, both_ref, weight_ref, small_ref):
    share = WIDTH // 128
    both = both_ref[0]
    for z in range(1, both_ref.shape[0]):
        both = both + both_ref[z]
    both = both * inverse_ref[0]
    for l in range(LB):
        weight_ref[:, l * 128 : (l + 1) * 128] = both[l * share : (l + 1) * share]
    for j in range(small_ref.shape[0]):
        small_ref[j] = both[LB * share : LB * share + 16]


def emit_kernel(small_ref, tap_ref, gain_ref, bias_ref):
    for l in range(LB):
        lanes = slice(l * 128, (l + 1) * 128)
        tap_ref[:, lanes] = small_ref[l * 40 : l * 40 + TAPS, :]
        gain_ref[:, lanes] = small_ref[l * 40 + TAPS : l * 40 + TAPS + 1, :]
        bias_ref[:, lanes] = small_ref[l * 40 + TAPS + 1 : l * 40 + TAPS + 2, :]


def valid_rows(length):
    return lax.broadcasted_iota(jnp.int32, (FR, 128), 0) < length


def forward_kernel(len_ref, core_ref, x_ref, stat_ref, gain_ref, bias_ref, tap_ref, tgt_ref,
                   keep_ref, send_ref, mpad_ref, slope_ref, mean_ref, rstd_ref, act_ref, term_ref, *, nz, ny):
    zero16 = jnp.zeros((16, 128), f32)
    for u in range(UTT):
        rows = pl.ds(u * FR, FR)
        sums = [stat_ref[2 * j : 2 * j + 1, rows] for j in range(4)]
        squares = [stat_ref[2 * j + 1 : 2 * j + 2, rows] for j in range(4)]
        mean = (sums[0] + sums[1] + sums[2] + sums[3]) * (1.0 / WIDTH)
        spread = squares[0] + squares[1] + squares[2] + squares[3]
        for s in sums:
            gap = s * (1.0 / CH) - mean
            spread = spread + CH * (gap * gap)
        rstd = lax.rsqrt(spread * (1.0 / WIDTH) + epsilon)
        mean_ref[u] = columns_of(mean)
        rstd_ref[u] = columns_of(rstd)

    def step(i, carry):
        u, l = i // LB, i % LB
        rows = pl.ds(pl.multiple_of(u * FR, FR), FR)
        lanes = pl.ds(pl.multiple_of(l * 128, 128), 128)
        keep = valid_rows(len_ref[u])
        normed = (x_ref[rows, lanes].astype(f32) - mean_ref[u]) * rstd_ref[u]
        masked = jnp.where(keep, normed * gain_ref[:, lanes] + bias_ref[:, lanes], 0.0)
        mpad_ref[i, 0:16, :] = zero16
        mpad_ref[i, 16 : 16 + FR, :] = masked
        mpad_ref[i, 16 + FR : PADDED, :] = zero16
        for r in range(0, FR, ROWS):
            acc = jnp.zeros((ROWS, 128), f32)
            for k in range(TAPS):
                acc = acc + tap_ref[k : k + 1, lanes] * mpad_ref[i, r + k + 1 : r + k + 1 + ROWS, :]
            gate = jax.nn.sigmoid(acc)
            slope_ref[i, r : r + ROWS, :] = gate * (1.0 + acc * (1.0 - gate))
            here = lax.broadcasted_iota(jnp.int32, (ROWS, 128), 0) + r < len_ref[u]
            act_ref[pl.ds(pl.multiple_of(u * FR + r, ROWS), ROWS), lanes] = jnp.where(
                here, acc * gate, 0.0
            ).astype(bf16)
        return carry

    lax.fori_loop(0, UTT * LB, step, 0)
    term_ref[...] = lax.dot_general(
        tgt_ref[...], act_ref[...], (((0,), (0,)), ((), ())), preferred_element_type=f32
    )
    is_first = core_ref[0] == 0
    share = WIDTH // (2 * nz * ny)
    for z in range(nz):
        for y in range(ny):
            source, goal = (z * ny + y) * 2 * share, (y * nz + z) * share
            first = term_ref[source : source + share, :]
            second = term_ref[source + share : source + 2 * share, :]
            keep_ref[goal : goal + share, :] = jnp.where(is_first, first, second)
            send_ref[goal : goal + share, :] = jnp.where(is_first, second, first)


def backward_kernel(len_ref, core_ref, x_ref, mean_ref, rstd_ref, gain_ref, tap_ref, tgt_ref, own_ref, other_ref, mpad_ref, slope_ref,
                    mgrad_ref, sums_ref, small_ref, agrad_ref, gpad_ref, hat_ref, dot_ref, part_ref, pw_ref, *, nz, ny):
    is_first = core_ref[0] == 0
    share = WIDTH // (2 * nz * ny)
    for y in range(ny):
        mine, its = own_ref[y].astype(f32), other_ref[y].astype(f32)
        part_ref[0] = jnp.where(is_first, mine, its)
        part_ref[1] = jnp.where(is_first, its, mine)
        for z in range(nz):
            for c in range(2):
                goal = ((z * ny + y) * 2 + c) * share
                pw_ref[goal : goal + share, :] = part_ref[c, z * share : (z + 1) * share, :]
    agrad_ref[...] = jnp.dot(tgt_ref[...], pw_ref[...].astype(bf16), preferred_element_type=f32)
    zero16 = jnp.zeros((16, 128), f32)
    gpad_ref[0:16, :] = zero16
    gpad_ref[16 + FR : PADDED, :] = zero16
    small_ref[...] = jnp.zeros(small_ref.shape, f32)

    def step(i, carry):
        u, l = i // LB, i % LB
        rows = pl.ds(pl.multiple_of(u * FR, FR), FR)
        lanes = pl.ds(pl.multiple_of(l * 128, 128), 128)
        keep = valid_rows(len_ref[u])
        gpad_ref[16 : 16 + FR, :] = jnp.where(keep, agrad_ref[rows, lanes] * slope_ref[i], 0.0)
        taps = [jnp.zeros((8, 128), f32) for _ in range(TAPS)]
        for r in range(0, FR, 8):
            grad = gpad_ref[16 + r : 24 + r, :]
            taps = [
                acc + grad * mpad_ref[i, r + k + 1 : r + k + 9, :] for k, acc in enumerate(taps)
            ]
        for k, acc in enumerate(taps):
            small_ref[pl.ds(l * 40 + k, 1), :] += jnp.sum(acc, axis=0, keepdims=True)
        gain_acc = jnp.zeros((ROWS, 128), f32)
        bias_acc = jnp.zeros((ROWS, 128), f32)
        first = l == 0
        for r in range(0, FR, ROWS):
            acc = jnp.zeros((ROWS, 128), f32)
            for k in range(TAPS):
                acc = acc + tap_ref[k : k + 1, lanes] * gpad_ref[r + 31 - k : r + 31 - k + ROWS, :]
            here = lax.broadcasted_iota(jnp.int32, (ROWS, 128), 0) + r < len_ref[u]
            acc = jnp.where(here, acc, 0.0)
            part = pl.ds(pl.multiple_of(u * FR + r, ROWS), ROWS)
            normed = (x_ref[part, lanes].astype(f32) - mean_ref[u, r : r + ROWS, :]) * rstd_ref[u, r : r + ROWS, :]
            gain_acc = gain_acc + acc * normed
            bias_acc = bias_acc + acc
            hat = acc * gain_ref[:, lanes]
            mgrad_ref[part, lanes] = hat
            hat_ref[u, r : r + ROWS, :] = jnp.where(first, 0.0, hat_ref[u, r : r + ROWS, :]) + hat
            dot_ref[u, r : r + ROWS, :] = jnp.where(first, 0.0, dot_ref[u, r : r + ROWS, :]) + hat * normed
        small_ref[pl.ds(l * 40 + 31, 1), :] += jnp.sum(gain_acc, axis=0, keepdims=True)
        small_ref[pl.ds(l * 40 + 32, 1), :] += jnp.sum(bias_acc, axis=0, keepdims=True)
        return carry

    lax.fori_loop(0, UTT * LB, step, 0)
    for u in range(UTT):
        rows = pl.ds(u * FR, FR)
        total, dot = rows_of(hat_ref[u]), rows_of(dot_ref[u])
        sums_ref[0:1, rows] = total
        sums_ref[1:2, rows] = dot


def finish_kernel(len_ref, own_ref, scale_ref, x_ref, mean_ref, rstd_ref, hat_ref, sums_ref, tgt_ref, out_ref):
    scale = scale_ref[0]
    for u in range(UTT):
        rows = pl.ds(u * FR, FR)
        keep = valid_rows(len_ref[u])
        total, dot = columns_of(sums_ref[0:1, rows] * (1.0 / WIDTH)), columns_of(sums_ref[1:2, rows] * (1.0 / WIDTH))
        for l in range(LB):
            lanes = pl.ds(l * 128, 128)
            normed = (x_ref[rows, lanes].astype(f32) - mean_ref[u]) * rstd_ref[u]
            grad = rstd_ref[u] * (hat_ref[rows, lanes] - total - normed * dot)
            own = tgt_ref[rows, pl.ds(pl.multiple_of(own_ref[0] * CH + l * 128, 128), 128)].astype(f32)
            out_ref[rows, lanes] = ((jnp.where(keep, own, 0.0) + grad) * scale).astype(bf16)


def kernel_call(kernel, micros, **options):
    return pl.pallas_call(
        kernel, cost_estimate=pl.CostEstimate(flops=0, transcendentals=0, bytes_accessed=micros * 3_000_000), **options
    )


def shape(*dims, dtype=f32):
    return jax.ShapeDtypeStruct(dims, dtype)


def swap(value):
    return lax.ppermute(value, "core", [(0, 1), (1, 0)])


def everyone(value, axis, count):
    return lax.all_to_all(jnp.broadcast_to(value, (count, *value.shape)), axis, 0, 0)


def program(frames_in, lengths, ln_gain, ln_bias, kernel, point_weight, target, *, nz, ny):
    core = lax.axis_index("core")
    place = lax.axis_index("x").reshape(1)
    gain, bias = ln_gain.reshape(1, CH), ln_bias.reshape(1, CH)
    out_rows = point_weight.shape[0]
    extra = jnp.pad(lengths.astype(bf16).reshape(1, UTT), ((0, 3), (0, CH - UTT)))
    own = jnp.concatenate([point_weight, extra], axis=0)
    by_z = everyone(own, "z", nz)
    own = kernel_call(
        pack_kernel, 1,
        out_shape=shape(ny, nz * out_rows + 16, CH, dtype=bf16),
        in_specs=[VMEM], out_specs=VMEM,
        scratch_shapes=[pltpu.VMEM((nz * out_rows + 16, CH), f32)],
    )(by_z)
    by_y = lax.all_to_all(own, "y", 0, 0)
    other_weight = swap(by_y)
    digits = (by_y[:, nz * out_rows, :128].astype(f32) + other_weight[:, nz * out_rows, :128].astype(f32)).sum(axis=0)
    frame_total = digits[0] * 256.0 + digits[1]
    inverse = 1.0 / frame_total

    stats = kernel_call(
        stats_kernel, 3, out_shape=shape(8, TOK), in_specs=[SMEM, VMEM], out_specs=VMEM
    )(place, frames_in)
    stats = lax.psum(stats, "x")
    half_rows = WIDTH // 2
    pieces = 2 * ny
    keep, send, mpad, slope, mean, rstd = kernel_call(
        functools.partial(forward_kernel, nz=nz, ny=ny), 10,
        out_shape=(
            shape(half_rows, CH),
            shape(half_rows, CH),
            shape(UTT * LB, PADDED, 128),
            shape(UTT * LB, FR, 128),
            shape(UTT, FR, 128),
            shape(UTT, FR, 128),
        ),
        in_specs=[SMEM, SMEM] + [VMEM] * 6,
        out_specs=[VMEM] * 6,
        scratch_shapes=[pltpu.VMEM((TOK, CH), bf16), pltpu.VMEM((WIDTH, CH), f32)],
    )(lengths, core.reshape(1), frames_in, stats, gain, bias, kernel, target)

    other = swap(send)
    term = (keep + other).reshape(ny, nz * out_rows, CH)
    term = lax.all_to_all(term, "y", 0, 0)
    hat, sums, small = kernel_call(
        functools.partial(backward_kernel, nz=nz, ny=ny), 16,
        out_shape=(shape(TOK, CH), shape(2, TOK), shape(pieces * 16, 128)),
        in_specs=[SMEM, SMEM] + [VMEM] * 10,
        out_specs=[VMEM] * 3,
        scratch_shapes=[
            pltpu.VMEM((TOK, CH), f32),
            pltpu.VMEM((PADDED, 128), f32),
            pltpu.VMEM((UTT, FR, 128), f32),
            pltpu.VMEM((UTT, FR, 128), f32),
            pltpu.VMEM((2, nz * out_rows + 16, CH), f32),
            pltpu.VMEM((WIDTH, CH), f32),
        ],
    )(lengths, core.reshape(1), frames_in, mean, rstd, gain, kernel, target, by_y, other_weight, mpad, slope)
    sums = lax.psum(sums, "x")
    frames_grad = kernel_call(
        finish_kernel, 5,
        out_shape=shape(TOK, CH, dtype=bf16),
        in_specs=[SMEM, SMEM, SMEM] + [VMEM] * 6,
        out_specs=VMEM,
    )(lengths, place, (TOK * 2 * ny * nz * inverse).reshape(1),
      frames_in, mean, rstd, hat, sums, target)

    small = lax.all_to_all(small.reshape(pieces, 16, 128), ("y", "core"), 0, 0)
    both = kernel_call(
        mix_kernel, 2, out_shape=shape(nz, out_rows * LB + 20, 128), in_specs=[VMEM] * 2, out_specs=VMEM
    )(term, small)
    both = lax.all_to_all(both, "z", 0, 0)
    weight_grad, small = kernel_call(
        unmix_kernel, 1,
        out_shape=(shape(out_rows, CH), shape(pieces, 16, 128)),
        in_specs=[SMEM, VMEM], out_specs=[VMEM] * 2,
    )(inverse.reshape(1), both)
    small = lax.all_to_all(small, ("y", "core"), 0, 0)
    tap_grad, gain_grad, bias_grad = kernel_call(
        emit_kernel, 1,
        out_shape=(shape(TAPS, CH), shape(1, CH), shape(1, CH)),
        in_specs=[VMEM], out_specs=[VMEM] * 3,
    )(small.reshape(pieces * 16, 128))
    return frames_grad, weight_grad, tap_grad, gain_grad.reshape(CH), bias_grad.reshape(CH)


def solution(mesh):
    nz, ny = 16, 4
    fine = Mesh(mesh.devices.reshape(nz, ny, 2, 4), ("z", "y", "core", "x"))
    dp = ("z", "y", "core")
    return jax.shard_map(
        functools.partial(program, nz=nz, ny=ny),
        mesh=fine,
        in_specs=(P(dp, "x"), P(dp), P("x"), P("x"), P(None, "x"), P(dp, "x"), P(dp, None)),
        out_specs=(P(dp, "x"), P(dp, "x"), P(None, "x"), P("x"), P("x")),
        check_vma=False,
    )
```

```python
import functools

import jax
import jax.numpy as jnp
from jax import lax
from jax.experimental import pallas as pl
from jax.experimental.pallas import tpu as pltpu
from jax.sharding import Mesh, PartitionSpec as P

epsilon = 1e-05
UTT = 4
FR = 256
TOK = UTT * FR
CH = 384
LB = CH // 128
TAPS = 31
HALF = 15
WIDTH = 1536
PADDED = FR + 32
ROWS = 32
f32 = jnp.float32
bf16 = jnp.bfloat16

VMEM = pl.BlockSpec(memory_space=pltpu.VMEM)
SMEM = pl.BlockSpec(memory_space=pltpu.SMEM)


def rows_of(column):
    return jnp.sum(column.T, axis=0, keepdims=True)


def columns_of(row):
    return jnp.broadcast_to(row, (128, FR)).T


def stats_kernel(own_ref, x_ref, out_ref):
    for u in range(UTT):
        rows = pl.ds(u * FR, FR)
        parts = [x_ref[rows, pl.ds(l * 128, 128)].astype(f32) for l in range(LB)]
        total = rows_of(parts[0] + parts[1] + parts[2])
        mean = columns_of(total * (1.0 / CH))
        parts = [p - mean for p in parts]
        square = rows_of(parts[0] * parts[0] + parts[1] * parts[1] + parts[2] * parts[2])
        for j in range(4):
            out_ref[2 * j : 2 * j + 1, rows] = jnp.where(own_ref[0] == j, total, 0.0)
            out_ref[2 * j + 1 : 2 * j + 2, rows] = jnp.where(own_ref[0] == j, square, 0.0)


def spread_kernel(len_ref, weight_ref, out_ref):
    share = weight_ref.shape[0]
    lane = lax.broadcasted_iota(jnp.int32, (16 - share, CH), 1)
    extra = jnp.zeros((16 - share, CH), f32)
    for u in range(UTT):
        extra = jnp.where(lane == u, len_ref[u].astype(f32), extra)
    both = jnp.concatenate([weight_ref[...].astype(f32), extra], axis=0).astype(bf16)
    for z in range(out_ref.shape[0]):
        out_ref[z] = both


def pack_kernel(part_ref, out_ref, rows_ref):
    nz, share = part_ref.shape[0], WIDTH // 128
    count = jnp.zeros((1, 128), f32)
    for z in range(nz):
        part = part_ref[z].astype(f32)
        rows_ref[z * share : (z + 1) * share, :] = part[:share]
        count = count + part[share : share + 1, :128]
    total = jnp.sum(count, axis=1, keepdims=True)
    high = jnp.floor(total * (1.0 / 256.0))
    spot = lax.broadcasted_iota(jnp.int32, (16, CH), 1) + CH * lax.broadcasted_iota(jnp.int32, (16, CH), 0)
    rows_ref[nz * share :, :] = jnp.where(spot == 0, high, jnp.where(spot == 1, total - high * 256.0, 0.0))
    packed = rows_ref[...].astype(bf16)
    for j in range(out_ref.shape[0]):
        out_ref[j] = packed


def mix_kernel(term_ref, small_ref, out_ref):
    nz, share = out_ref.shape[0], WIDTH // 128
    small = small_ref[0]
    for j in range(1, small_ref.shape[0]):
        small = small + small_ref[j]
    for z in range(nz):
        rows = term_ref[0, z * share : (z + 1) * share, :]
        for j in range(1, term_ref.shape[0]):
            rows = rows + term_ref[j, z * share : (z + 1) * share, :]
        for l in range(LB):
            out_ref[z, l * share : (l + 1) * share, :] = rows[:, l * 128 : (l + 1) * 128]
        out_ref[z, LB * share : LB * share + 16, :] = small
        out_ref[z, LB * share + 16 :, :] = jnp.zeros((4, 128), f32)


def unmix_kernel(inverse_ref, both_ref, weight_ref, small_ref):
    share = WIDTH // 128
    both = both_ref[0]
    for z in range(1, both_ref.shape[0]):
        both = both + both_ref[z]
    both = both * inverse_ref[0]
    for l in range(LB):
        weight_ref[:, l * 128 : (l + 1) * 128] = both[l * share : (l + 1) * share]
    for j in range(small_ref.shape[0]):
        small_ref[j] = both[LB * share : LB * share + 16]


def emit_kernel(small_ref, tap_ref, gain_ref, bias_ref):
    for l in range(LB):
        lanes = slice(l * 128, (l + 1) * 128)
        tap_ref[:, lanes] = small_ref[l * 40 : l * 40 + TAPS, :]
        gain_ref[lanes] = small_ref[l * 40 + TAPS, :]
        bias_ref[lanes] = small_ref[l * 40 + TAPS + 1, :]


def valid_rows(length):
    return lax.broadcasted_iota(jnp.int32, (FR, 128), 0) < length


def forward_kernel(len_ref, core_ref, x_ref, stat_ref, gain_ref, bias_ref, tap_ref, tgt_ref,
                   keep_ref, send_ref, npad_ref, slope_ref, mean_ref, rstd_ref, act_ref, term_ref, mpad_ref, par_ref, *, nz, ny):
    zero16 = jnp.zeros((16, 128), f32)
    par_ref[0:1, :] = gain_ref[...].reshape(1, CH)
    par_ref[1:2, :] = bias_ref[...].reshape(1, CH)
    mpad_ref[0:16, :] = zero16
    mpad_ref[16 + FR : PADDED, :] = zero16
    for u in range(UTT):
        rows = pl.ds(u * FR, FR)
        sums = [stat_ref[2 * j : 2 * j + 1, rows] for j in range(4)]
        squares = [stat_ref[2 * j + 1 : 2 * j + 2, rows] for j in range(4)]
        mean = (sums[0] + sums[1] + sums[2] + sums[3]) * (1.0 / WIDTH)
        spread = squares[0] + squares[1] + squares[2] + squares[3]
        for s in sums:
            gap = s * (1.0 / CH) - mean
            spread = spread + CH * (gap * gap)
        rstd = lax.rsqrt(spread * (1.0 / WIDTH) + epsilon)
        mean_ref[u] = columns_of(mean)
        rstd_ref[u] = columns_of(rstd)

    def step(i, carry):
        u, l = i // LB, i % LB
        rows = pl.ds(pl.multiple_of(u * FR, FR), FR)
        lanes = pl.ds(pl.multiple_of(l * 128, 128), 128)
        keep = valid_rows(len_ref[u])
        normed = (x_ref[rows, lanes].astype(f32) - mean_ref[u]) * rstd_ref[u]
        mpad_ref[16 : 16 + FR, :] = jnp.where(keep, normed * par_ref[0:1, lanes] + par_ref[1:2, lanes], 0.0)
        npad_ref[i, 0:16, :] = zero16
        npad_ref[i, 16 : 16 + FR, :] = jnp.where(keep, normed, 0.0)
        npad_ref[i, 16 + FR : PADDED, :] = zero16
        for r in range(0, FR, ROWS):
            acc = jnp.zeros((ROWS, 128), f32)
            for k in range(TAPS):
                acc = acc + tap_ref[k : k + 1, lanes] * mpad_ref[r + k + 1 : r + k + 1 + ROWS, :]
            gate = jax.nn.sigmoid(acc)
            slope_ref[i, r : r + ROWS, :] = gate * (1.0 + acc * (1.0 - gate))
            here = lax.broadcasted_iota(jnp.int32, (ROWS, 128), 0) + r < len_ref[u]
            act_ref[pl.ds(pl.multiple_of(u * FR + r, ROWS), ROWS), lanes] = jnp.where(
                here, acc * gate, 0.0
            ).astype(bf16)
        return carry

    lax.fori_loop(0, UTT * LB, step, 0)
    term_ref[...] = lax.dot_general(
        tgt_ref[...], act_ref[...], (((0,), (0,)), ((), ())), preferred_element_type=f32
    )
    is_first = core_ref[0] == 0
    share = WIDTH // (2 * nz * ny)
    for z in range(nz):
        for y in range(ny):
            source, goal = (z * ny + y) * 2 * share, (y * nz + z) * share
            first = term_ref[source : source + share, :]
            second = term_ref[source + share : source + 2 * share, :]
            keep_ref[goal : goal + share, :] = jnp.where(is_first, first, second)
            send_ref[goal : goal + share, :] = jnp.where(is_first, second, first)


def backward_kernel(len_ref, core_ref, gain_ref, bias_ref, tap_ref, tgt_ref, own_ref, other_ref, npad_ref, slope_ref,
                    gpad_ref, small_ref, agrad_ref, part_ref, pw_ref, q_ref, s_ref, par_ref, *, nz, ny):
    is_first = core_ref[0] == 0
    share = WIDTH // (2 * nz * ny)
    for y in range(ny):
        mine, its = own_ref[y].astype(f32), other_ref[y].astype(f32)
        part_ref[0] = jnp.where(is_first, mine, its)
        part_ref[1] = jnp.where(is_first, its, mine)
        for z in range(nz):
            for c in range(2):
                goal = ((z * ny + y) * 2 + c) * share
                pw_ref[goal : goal + share, :] = part_ref[c, z * share : (z + 1) * share, :]
    agrad_ref[...] = jnp.dot(tgt_ref[...], pw_ref[...].astype(bf16), preferred_element_type=f32)
    par_ref[0:1, :] = gain_ref[...].reshape(1, CH)
    par_ref[1:2, :] = bias_ref[...].reshape(1, CH)
    zero16 = jnp.zeros((16, 128), f32)
    q_ref[...] = jnp.zeros(q_ref.shape, f32)
    s_ref[...] = jnp.zeros(s_ref.shape, f32)

    def step(i, carry):
        u, l = i // LB, i % LB
        rows = pl.ds(pl.multiple_of(u * FR, FR), FR)
        lanes = pl.ds(pl.multiple_of(l * 128, 128), 128)
        keep = valid_rows(len_ref[u])
        gpad_ref[i, 0:16, :] = zero16
        gpad_ref[i, 16 + FR : PADDED, :] = zero16
        gpad_ref[i, 16 : 16 + FR, :] = jnp.where(keep, agrad_ref[rows, lanes] * slope_ref[i], 0.0)
        taps = [jnp.zeros((8, 128), f32) for _ in range(TAPS)]
        total = jnp.zeros((8, 128), f32)
        for r in range(0, FR, 8):
            grad = gpad_ref[i, 16 + r : 24 + r, :]
            total = total + grad
            taps = [acc + grad * npad_ref[i, r + k + 1 : r + k + 9, :] for k, acc in enumerate(taps)]
        for k, acc in enumerate(taps):
            q_ref[l, k : k + 1, :] += jnp.sum(acc, axis=0, keepdims=True)
        total = jnp.sum(total, axis=0, keepdims=True)
        head = gpad_ref[i, 16:32, :]
        tail = gpad_ref[i, pl.ds(len_ref[u], 16), :]
        row = lax.broadcasted_iota(jnp.int32, (16, 128), 0)
        s_ref[l, HALF : HALF + 1, :] += total
        for j in range(1, HALF + 1):
            first = jnp.sum(jnp.where(row < j, head, 0.0), axis=0, keepdims=True)
            last = jnp.sum(jnp.where(row >= 16 - j, tail, 0.0), axis=0, keepdims=True)
            s_ref[l, HALF - j : HALF - j + 1, :] += total - first
            s_ref[l, HALF + j : HALF + j + 1, :] += total - last
        return carry

    lax.fori_loop(0, UTT * LB, step, 0)
    small_ref[...] = jnp.zeros(small_ref.shape, f32)
    for l in range(LB):
        lanes = slice(l * 128, (l + 1) * 128)
        q, s, w = q_ref[l, :TAPS, :], s_ref[l, :TAPS, :], tap_ref[:, lanes]
        small_ref[l * 40 : l * 40 + TAPS, :] = par_ref[0:1, lanes] * q + par_ref[1:2, lanes] * s
        small_ref[l * 40 + TAPS : l * 40 + TAPS + 1, :] = jnp.sum(w * q, axis=0, keepdims=True)
        small_ref[l * 40 + TAPS + 1 : l * 40 + TAPS + 2, :] = jnp.sum(w * s, axis=0, keepdims=True)


def input_kernel(len_ref, x_ref, mean_ref, rstd_ref, gain_ref, tap_ref, gpad_ref,
                 mgrad_ref, sums_ref, hat_ref, dot_ref, par_ref):
    par_ref[...] = gain_ref[...].reshape(1, CH)

    def step(i, carry):
        u, l = i // LB, i % LB
        lanes = pl.ds(pl.multiple_of(l * 128, 128), 128)
        first = l == 0
        for r in range(0, FR, ROWS):
            acc = jnp.zeros((ROWS, 128), f32)
            for k in range(TAPS):
                acc = acc + tap_ref[k : k + 1, lanes] * gpad_ref[i, r + 31 - k : r + 31 - k + ROWS, :]
            here = lax.broadcasted_iota(jnp.int32, (ROWS, 128), 0) + r < len_ref[u]
            hat = jnp.where(here, acc, 0.0) * par_ref[:, lanes]
            part = pl.ds(pl.multiple_of(u * FR + r, ROWS), ROWS)
            normed = (x_ref[part, lanes].astype(f32) - mean_ref[u, r : r + ROWS, :]) * rstd_ref[u, r : r + ROWS, :]
            mgrad_ref[part, lanes] = hat
            hat_ref[u, r : r + ROWS, :] = jnp.where(first, 0.0, hat_ref[u, r : r + ROWS, :]) + hat
            dot_ref[u, r : r + ROWS, :] = jnp.where(first, 0.0, dot_ref[u, r : r + ROWS, :]) + hat * normed
        return carry

    lax.fori_loop(0, UTT * LB, step, 0)
    for u in range(UTT):
        rows = pl.ds(u * FR, FR)
        sums_ref[0:1, rows] = rows_of(hat_ref[u])
        sums_ref[1:2, rows] = rows_of(dot_ref[u])


def finish_kernel(len_ref, own_ref, scale_ref, x_ref, mean_ref, rstd_ref, hat_ref, sums_ref, tgt_ref, out_ref):
    scale = scale_ref[0]
    for u in range(UTT):
        rows = pl.ds(u * FR, FR)
        keep = valid_rows(len_ref[u])
        total, dot = columns_of(sums_ref[0:1, rows] * (1.0 / WIDTH)), columns_of(sums_ref[1:2, rows] * (1.0 / WIDTH))
        for l in range(LB):
            lanes = pl.ds(l * 128, 128)
            normed = (x_ref[rows, lanes].astype(f32) - mean_ref[u]) * rstd_ref[u]
            grad = rstd_ref[u] * (hat_ref[rows, lanes] - total - normed * dot)
            own = tgt_ref[rows, pl.ds(pl.multiple_of(own_ref[0] * CH + l * 128, 128), 128)].astype(f32)
            out_ref[rows, lanes] = ((jnp.where(keep, own, 0.0) + grad) * scale).astype(bf16)


def kernel_call(kernel, micros, **options):
    return pl.pallas_call(
        kernel, cost_estimate=pl.CostEstimate(flops=0, transcendentals=0, bytes_accessed=micros * 3_000_000), **options
    )


def shape(*dims, dtype=f32):
    return jax.ShapeDtypeStruct(dims, dtype)


def swap(value):
    return lax.ppermute(value, "core", [(0, 1), (1, 0)])


def program(frames_in, lengths, ln_gain, ln_bias, kernel, point_weight, target, *, nz, ny):
    core = lax.axis_index("core")
    place = lax.axis_index("x").reshape(1)
    out_rows = point_weight.shape[0]
    own = kernel_call(
        spread_kernel, 1, out_shape=shape(nz, 16, CH, dtype=bf16), in_specs=[SMEM, VMEM], out_specs=VMEM
    )(lengths, point_weight)
    by_z = lax.all_to_all(own, "z", 0, 0)
    own = kernel_call(
        pack_kernel, 1,
        out_shape=shape(ny, nz * out_rows + 16, CH, dtype=bf16),
        in_specs=[VMEM], out_specs=VMEM,
        scratch_shapes=[pltpu.VMEM((nz * out_rows + 16, CH), f32)],
    )(by_z)
    by_y = lax.all_to_all(own, "y", 0, 0)
    other_weight = swap(by_y)
    digits = (by_y[:, nz * out_rows, :128].astype(f32) + other_weight[:, nz * out_rows, :128].astype(f32)).sum(axis=0)
    frame_total = digits[0] * 256.0 + digits[1]
    inverse = 1.0 / frame_total

    stats = kernel_call(
        stats_kernel, 3, out_shape=shape(8, TOK), in_specs=[SMEM, VMEM], out_specs=VMEM
    )(place, frames_in)
    stats = lax.psum(stats, "x")
    half_rows = WIDTH // 2
    pieces = 2 * ny
    keep, send, npad, slope, mean, rstd = kernel_call(
        functools.partial(forward_kernel, nz=nz, ny=ny), 10,
        out_shape=(
            shape(half_rows, CH),
            shape(half_rows, CH),
            shape(UTT * LB, PADDED, 128),
            shape(UTT * LB, FR, 128),
            shape(UTT, FR, 128),
            shape(UTT, FR, 128),
        ),
        in_specs=[SMEM, SMEM] + [VMEM] * 6,
        out_specs=[VMEM] * 6,
        scratch_shapes=[
            pltpu.VMEM((TOK, CH), bf16),
            pltpu.VMEM((WIDTH, CH), f32),
            pltpu.VMEM((PADDED, 128), f32),
            pltpu.VMEM((2, CH), f32),
        ],
    )(lengths, core.reshape(1), frames_in, stats, ln_gain, ln_bias, kernel, target)

    other = swap(send)
    term = (keep + other).reshape(ny, nz * out_rows, CH)
    term = lax.all_to_all(term, "y", 0, 0)
    gpad, small = kernel_call(
        functools.partial(backward_kernel, nz=nz, ny=ny), 10,
        out_shape=(shape(UTT * LB, PADDED, 128), shape(pieces * 16, 128)),
        in_specs=[SMEM, SMEM] + [VMEM] * 8,
        out_specs=[VMEM] * 2,
        scratch_shapes=[
            pltpu.VMEM((TOK, CH), f32),
            pltpu.VMEM((2, nz * out_rows + 16, CH), f32),
            pltpu.VMEM((WIDTH, CH), f32),
            pltpu.VMEM((LB, 32, 128), f32),
            pltpu.VMEM((LB, 32, 128), f32),
            pltpu.VMEM((2, CH), f32),
        ],
    )(lengths, core.reshape(1), ln_gain, ln_bias, kernel, target, by_y, other_weight, npad, slope)
    hat, sums = kernel_call(
        input_kernel, 8,
        out_shape=(shape(TOK, CH), shape(2, TOK)),
        in_specs=[SMEM] + [VMEM] * 6,
        out_specs=[VMEM] * 2,
        scratch_shapes=[
            pltpu.VMEM((UTT, FR, 128), f32),
            pltpu.VMEM((UTT, FR, 128), f32),
            pltpu.VMEM((1, CH), f32),
        ],
    )(lengths, frames_in, mean, rstd, ln_gain, kernel, gpad)
    sums = lax.psum(sums, "x")
    frames_grad = kernel_call(
        finish_kernel, 5,
        out_shape=shape(TOK, CH, dtype=bf16),
        in_specs=[SMEM, SMEM, SMEM] + [VMEM] * 6,
        out_specs=VMEM,
    )(lengths, place, (TOK * 2 * ny * nz * inverse).reshape(1),
      frames_in, mean, rstd, hat, sums, target)

    small = lax.all_to_all(small.reshape(pieces, 16, 128), ("y", "core"), 0, 0)
    both = kernel_call(
        mix_kernel, 2, out_shape=shape(nz, out_rows * LB + 20, 128), in_specs=[VMEM] * 2, out_specs=VMEM
    )(term, small)
    both = lax.all_to_all(both, "z", 0, 0)
    weight_grad, small = kernel_call(
        unmix_kernel, 1,
        out_shape=(shape(out_rows, CH), shape(pieces, 16, 128)),
        in_specs=[SMEM, VMEM], out_specs=[VMEM] * 2,
    )(inverse.reshape(1), both)
    small = lax.all_to_all(small, ("y", "core"), 0, 0)
    tap_grad, gain_grad, bias_grad = kernel_call(
        emit_kernel, 1,
        out_shape=(shape(TAPS, CH), shape(CH), shape(CH)),
        in_specs=[VMEM], out_specs=[VMEM] * 3,
    )(small.reshape(pieces * 16, 128))
    return frames_grad, weight_grad, tap_grad, gain_grad, bias_grad


def solution(mesh):
    nz, ny = 16, 4
    fine = Mesh(mesh.devices.reshape(nz, ny, 2, 4), ("z", "y", "core", "x"))
    dp = ("z", "y", "core")
    return jax.shard_map(
        functools.partial(program, nz=nz, ny=ny),
        mesh=fine,
        in_specs=(P(dp, "x"), P(dp), P("x"), P("x"), P(None, "x"), P(dp, "x"), P(dp, None)),
        out_specs=(P(dp, "x"), P(dp, "x"), P(None, "x"), P("x"), P("x")),
        check_vma=False,
    )
```

```python
import functools

import jax
import jax.numpy as jnp
from jax import lax
from jax.experimental import pallas as pl
from jax.experimental.pallas import tpu as pltpu
from jax.sharding import Mesh, PartitionSpec as P

epsilon = 1e-05
UTT = 4
FR = 256
TOK = UTT * FR
CH = 384
LB = CH // 128
TAPS = 31
HALF = 15
WIDTH = 1536
PADDED = FR + 32
ROWS = 32
f32 = jnp.float32
bf16 = jnp.bfloat16

VMEM = pl.BlockSpec(memory_space=pltpu.VMEM)
ANY = pl.BlockSpec(memory_space=pl.ANY)
SMEM = pl.BlockSpec(memory_space=pltpu.SMEM)


def rows_of(column):
    return jnp.sum(column.T, axis=0, keepdims=True)


def columns_of(row):
    return jnp.broadcast_to(row, (128, FR)).T


def stats_kernel(own_ref, x_ref, out_ref):
    for u in range(UTT):
        rows = pl.ds(u * FR, FR)
        parts = [x_ref[rows, pl.ds(l * 128, 128)].astype(f32) for l in range(LB)]
        total = rows_of(parts[0] + parts[1] + parts[2])
        mean = columns_of(total * (1.0 / CH))
        parts = [p - mean for p in parts]
        square = rows_of(parts[0] * parts[0] + parts[1] * parts[1] + parts[2] * parts[2])
        for j in range(4):
            out_ref[2 * j : 2 * j + 1, rows] = jnp.where(own_ref[0] == j, total, 0.0)
            out_ref[2 * j + 1 : 2 * j + 2, rows] = jnp.where(own_ref[0] == j, square, 0.0)


def spread_kernel(len_ref, weight_ref, out_ref):
    share = weight_ref.shape[0]
    lane = lax.broadcasted_iota(jnp.int32, (16 - share, CH), 1)
    extra = jnp.zeros((16 - share, CH), f32)
    for u in range(UTT):
        extra = jnp.where(lane == u, len_ref[u].astype(f32), extra)
    both = jnp.concatenate([weight_ref[...].astype(f32), extra], axis=0).astype(bf16)
    for z in range(out_ref.shape[0]):
        out_ref[z] = both


def mix_kernel(term_ref, out_ref):
    nz, share = out_ref.shape[0], WIDTH // 128
    for z in range(nz):
        rows = term_ref[0, z * share : (z + 1) * share, :]
        for j in range(1, term_ref.shape[0]):
            rows = rows + term_ref[j, z * share : (z + 1) * share, :]
        out_ref[z, 0:16, :] = jnp.zeros((16, 128), f32)
        for l in range(LB):
            out_ref[z, 16 + l * share : 16 + (l + 1) * share, :] = rows[:, l * 128 : (l + 1) * 128]
        out_ref[z, 16 + LB * share :, :] = jnp.zeros((4, 128), f32)


def fill_kernel(small_ref, both_ref, out_ref, sum_ref, sem_ref):
    small = small_ref[0]
    for j in range(1, small_ref.shape[0]):
        small = small + small_ref[j]
    sum_ref[...] = small
    copies = [
        pltpu.make_async_copy(sum_ref, out_ref.at[z, 0:16, :], sem_ref.at[z]) for z in range(out_ref.shape[0])
    ]
    for copy in copies:
        copy.start()
    for copy in copies:
        copy.wait()


def unmix_kernel(inverse_ref, both_ref, weight_ref, small_ref):
    share = WIDTH // 128
    both = both_ref[0]
    for z in range(1, both_ref.shape[0]):
        both = both + both_ref[z]
    both = both * inverse_ref[0]
    for l in range(LB):
        weight_ref[:, l * 128 : (l + 1) * 128] = both[16 + l * share : 16 + (l + 1) * share]
    for j in range(small_ref.shape[0]):
        small_ref[j] = both[:16]


def emit_kernel(small_ref, tap_ref, gain_ref, bias_ref):
    for l in range(LB):
        lanes = slice(l * 128, (l + 1) * 128)
        tap_ref[:, lanes] = small_ref[l * 40 : l * 40 + TAPS, :]
        gain_ref[lanes] = small_ref[l * 40 + TAPS, :]
        bias_ref[lanes] = small_ref[l * 40 + TAPS + 1, :]


def valid_rows(length):
    return lax.broadcasted_iota(jnp.int32, (FR, 128), 0) < length


def forward_kernel(len_ref, core_ref, x_ref, stat_ref, gain_ref, bias_ref, tap_ref, tgt_ref,
                   keep_ref, send_ref, npad_ref, slope_ref, mean_ref, rstd_ref, act_ref, term_ref, mpad_ref, par_ref, *, nz, ny):
    zero16 = jnp.zeros((16, 128), f32)
    par_ref[0:1, :] = gain_ref[...].reshape(1, CH)
    par_ref[1:2, :] = bias_ref[...].reshape(1, CH)
    mpad_ref[0:16, :] = zero16
    mpad_ref[16 + FR : PADDED, :] = zero16
    for u in range(UTT):
        rows = pl.ds(u * FR, FR)
        sums = [stat_ref[2 * j : 2 * j + 1, rows] for j in range(4)]
        squares = [stat_ref[2 * j + 1 : 2 * j + 2, rows] for j in range(4)]
        mean = (sums[0] + sums[1] + sums[2] + sums[3]) * (1.0 / WIDTH)
        spread = squares[0] + squares[1] + squares[2] + squares[3]
        for s in sums:
            gap = s * (1.0 / CH) - mean
            spread = spread + CH * (gap * gap)
        rstd = lax.rsqrt(spread * (1.0 / WIDTH) + epsilon)
        mean_ref[u] = columns_of(mean)
        rstd_ref[u] = columns_of(rstd)

    def step(i, carry):
        u, l = i // LB, i % LB
        rows = pl.ds(pl.multiple_of(u * FR, FR), FR)
        lanes = pl.ds(pl.multiple_of(l * 128, 128), 128)
        keep = valid_rows(len_ref[u])
        normed = (x_ref[rows, lanes].astype(f32) - mean_ref[u]) * rstd_ref[u]
        mpad_ref[16 : 16 + FR, :] = jnp.where(keep, normed * par_ref[0:1, lanes] + par_ref[1:2, lanes], 0.0)
        npad_ref[i, 0:16, :] = zero16
        npad_ref[i, 16 : 16 + FR, :] = jnp.where(keep, normed, 0.0)
        npad_ref[i, 16 + FR : PADDED, :] = zero16
        for r in range(0, FR, ROWS):
            acc = jnp.zeros((ROWS, 128), f32)
            for k in range(TAPS):
                acc = acc + tap_ref[k : k + 1, lanes] * mpad_ref[r + k + 1 : r + k + 1 + ROWS, :]
            gate = jax.nn.sigmoid(acc)
            slope_ref[i, r : r + ROWS, :] = gate * (1.0 + acc * (1.0 - gate))
            here = lax.broadcasted_iota(jnp.int32, (ROWS, 128), 0) + r < len_ref[u]
            act_ref[pl.ds(pl.multiple_of(u * FR + r, ROWS), ROWS), lanes] = jnp.where(
                here, acc * gate, 0.0
            ).astype(bf16)
        return carry

    lax.fori_loop(0, UTT * LB, step, 0)
    term_ref[...] = lax.dot_general(
        tgt_ref[...], act_ref[...], (((0,), (0,)), ((), ())), preferred_element_type=f32
    )
    is_first = core_ref[0] == 0
    share = WIDTH // (2 * nz * ny)
    for z in range(nz):
        for y in range(ny):
            source, goal = (z * ny + y) * 2 * share, (y * nz + z) * share
            first = term_ref[source : source + share, :]
            second = term_ref[source + share : source + 2 * share, :]
            keep_ref[goal : goal + share, :] = jnp.where(is_first, first, second)
            send_ref[goal : goal + share, :] = jnp.where(is_first, second, first)


def backward_kernel(len_ref, core_ref, gain_ref, bias_ref, tap_ref, tgt_ref, own_ref, other_ref, npad_ref, slope_ref,
                    gpad_ref, small_ref, agrad_ref, pw_ref, q_ref, s_ref, par_ref, *, nz, ny):
    is_first = core_ref[0] == 0
    share = WIDTH // (2 * nz * ny)
    for y in range(ny):
        for z in range(nz):
            mine, its = own_ref[y, z].astype(f32)[:share], other_ref[y, z].astype(f32)[:share]
            goal = (z * ny + y) * 2 * share
            pw_ref[goal : goal + share, :] = jnp.where(is_first, mine, its)
            pw_ref[goal + share : goal + 2 * share, :] = jnp.where(is_first, its, mine)
    agrad_ref[...] = jnp.dot(tgt_ref[...], pw_ref[...].astype(bf16), preferred_element_type=f32)
    par_ref[0:1, :] = gain_ref[...].reshape(1, CH)
    par_ref[1:2, :] = bias_ref[...].reshape(1, CH)
    zero16 = jnp.zeros((16, 128), f32)
    q_ref[...] = jnp.zeros(q_ref.shape, f32)
    s_ref[...] = jnp.zeros(s_ref.shape, f32)

    def step(i, carry):
        u, l = i // LB, i % LB
        rows = pl.ds(pl.multiple_of(u * FR, FR), FR)
        lanes = pl.ds(pl.multiple_of(l * 128, 128), 128)
        keep = valid_rows(len_ref[u])
        gpad_ref[i, 0:16, :] = zero16
        gpad_ref[i, 16 + FR : PADDED, :] = zero16
        gpad_ref[i, 16 : 16 + FR, :] = jnp.where(keep, agrad_ref[rows, lanes] * slope_ref[i], 0.0)
        taps = [jnp.zeros((8, 128), f32) for _ in range(TAPS)]
        total = jnp.zeros((8, 128), f32)
        for r in range(0, FR, 8):
            grad = gpad_ref[i, 16 + r : 24 + r, :]
            total = total + grad
            taps = [acc + grad * npad_ref[i, r + k + 1 : r + k + 9, :] for k, acc in enumerate(taps)]
        for k, acc in enumerate(taps):
            q_ref[l, k : k + 1, :] += jnp.sum(acc, axis=0, keepdims=True)
        total = jnp.sum(total, axis=0, keepdims=True)
        head = gpad_ref[i, 16:32, :]
        tail = gpad_ref[i, pl.ds(len_ref[u], 16), :]
        row = lax.broadcasted_iota(jnp.int32, (16, 128), 0)
        s_ref[l, HALF : HALF + 1, :] += total
        for j in range(1, HALF + 1):
            first = jnp.sum(jnp.where(row < j, head, 0.0), axis=0, keepdims=True)
            last = jnp.sum(jnp.where(row >= 16 - j, tail, 0.0), axis=0, keepdims=True)
            s_ref[l, HALF - j : HALF - j + 1, :] += total - first
            s_ref[l, HALF + j : HALF + j + 1, :] += total - last
        return carry

    lax.fori_loop(0, UTT * LB, step, 0)
    small_ref[...] = jnp.zeros(small_ref.shape, f32)
    for l in range(LB):
        lanes = slice(l * 128, (l + 1) * 128)
        q, s, w = q_ref[l, :TAPS, :], s_ref[l, :TAPS, :], tap_ref[:, lanes]
        small_ref[l * 40 : l * 40 + TAPS, :] = par_ref[0:1, lanes] * q + par_ref[1:2, lanes] * s
        small_ref[l * 40 + TAPS : l * 40 + TAPS + 1, :] = jnp.sum(w * q, axis=0, keepdims=True)
        small_ref[l * 40 + TAPS + 1 : l * 40 + TAPS + 2, :] = jnp.sum(w * s, axis=0, keepdims=True)


def input_kernel(len_ref, x_ref, mean_ref, rstd_ref, gain_ref, tap_ref, gpad_ref,
                 mgrad_ref, sums_ref, hat_ref, dot_ref, par_ref):
    par_ref[...] = gain_ref[...].reshape(1, CH)

    def step(i, carry):
        u, l = i // LB, i % LB
        lanes = pl.ds(pl.multiple_of(l * 128, 128), 128)
        first = l == 0
        for r in range(0, FR, ROWS):
            acc = jnp.zeros((ROWS, 128), f32)
            for k in range(TAPS):
                acc = acc + tap_ref[k : k + 1, lanes] * gpad_ref[i, r + 31 - k : r + 31 - k + ROWS, :]
            here = lax.broadcasted_iota(jnp.int32, (ROWS, 128), 0) + r < len_ref[u]
            hat = jnp.where(here, acc, 0.0) * par_ref[:, lanes]
            part = pl.ds(pl.multiple_of(u * FR + r, ROWS), ROWS)
            normed = (x_ref[part, lanes].astype(f32) - mean_ref[u, r : r + ROWS, :]) * rstd_ref[u, r : r + ROWS, :]
            mgrad_ref[part, lanes] = hat
            hat_ref[u, r : r + ROWS, :] = jnp.where(first, 0.0, hat_ref[u, r : r + ROWS, :]) + hat
            dot_ref[u, r : r + ROWS, :] = jnp.where(first, 0.0, dot_ref[u, r : r + ROWS, :]) + hat * normed
        return carry

    lax.fori_loop(0, UTT * LB, step, 0)
    for u in range(UTT):
        rows = pl.ds(u * FR, FR)
        sums_ref[0:1, rows] = rows_of(hat_ref[u])
        sums_ref[1:2, rows] = rows_of(dot_ref[u])


def finish_kernel(len_ref, own_ref, scale_ref, x_ref, mean_ref, rstd_ref, hat_ref, sums_ref, tgt_ref, out_ref):
    scale = scale_ref[0]
    for u in range(UTT):
        rows = pl.ds(u * FR, FR)
        keep = valid_rows(len_ref[u])
        total, dot = columns_of(sums_ref[0:1, rows] * (1.0 / WIDTH)), columns_of(sums_ref[1:2, rows] * (1.0 / WIDTH))
        for l in range(LB):
            lanes = pl.ds(l * 128, 128)
            normed = (x_ref[rows, lanes].astype(f32) - mean_ref[u]) * rstd_ref[u]
            grad = rstd_ref[u] * (hat_ref[rows, lanes] - total - normed * dot)
            own = tgt_ref[rows, pl.ds(pl.multiple_of(own_ref[0] * CH + l * 128, 128), 128)].astype(f32)
            out_ref[rows, lanes] = ((jnp.where(keep, own, 0.0) + grad) * scale).astype(bf16)


def kernel_call(kernel, micros, **options):
    return pl.pallas_call(
        kernel, cost_estimate=pl.CostEstimate(flops=0, transcendentals=0, bytes_accessed=micros * 3_000_000), **options
    )


def shape(*dims, dtype=f32):
    return jax.ShapeDtypeStruct(dims, dtype)


def swap(value):
    return lax.ppermute(value, "core", [(0, 1), (1, 0)])


def everyone(value, axis, count):
    return lax.all_to_all(jnp.broadcast_to(value, (count, *value.shape)), axis, 0, 0)


def program(frames_in, lengths, ln_gain, ln_bias, kernel, point_weight, target, *, nz, ny):
    core = lax.axis_index("core")
    place = lax.axis_index("x").reshape(1)
    out_rows = point_weight.shape[0]
    own = kernel_call(
        spread_kernel, 1, out_shape=shape(nz, 16, CH, dtype=bf16), in_specs=[SMEM, VMEM], out_specs=VMEM
    )(lengths, point_weight)
    by_z = lax.all_to_all(own, "z", 0, 0)
    by_y = everyone(by_z, "y", ny)
    other_weight = swap(by_y)
    frame_total = jnp.sum(by_y[:, :, out_rows, :UTT].astype(f32) + other_weight[:, :, out_rows, :UTT].astype(f32))
    inverse = 1.0 / frame_total

    stats = kernel_call(
        stats_kernel, 3, out_shape=shape(8, TOK), in_specs=[SMEM, VMEM], out_specs=VMEM
    )(place, frames_in)
    stats = lax.psum(stats, "x")
    half_rows = WIDTH // 2
    pieces = 2 * ny
    keep, send, npad, slope, mean, rstd = kernel_call(
        functools.partial(forward_kernel, nz=nz, ny=ny), 10,
        out_shape=(
            shape(half_rows, CH),
            shape(half_rows, CH),
            shape(UTT * LB, PADDED, 128),
            shape(UTT * LB, FR, 128),
            shape(UTT, FR, 128),
            shape(UTT, FR, 128),
        ),
        in_specs=[SMEM, SMEM] + [VMEM] * 6,
        out_specs=[VMEM] * 6,
        scratch_shapes=[
            pltpu.VMEM((TOK, CH), bf16),
            pltpu.VMEM((WIDTH, CH), f32),
            pltpu.VMEM((PADDED, 128), f32),
            pltpu.VMEM((2, CH), f32),
        ],
    )(lengths, core.reshape(1), frames_in, stats, ln_gain, ln_bias, kernel, target)

    other = swap(send)
    term = (keep + other).reshape(ny, nz * out_rows, CH)
    term = lax.all_to_all(term, "y", 0, 0)
    gpad, small = kernel_call(
        functools.partial(backward_kernel, nz=nz, ny=ny), 10,
        out_shape=(shape(UTT * LB, PADDED, 128), shape(pieces * 16, 128)),
        in_specs=[SMEM, SMEM] + [VMEM] * 8,
        out_specs=[VMEM] * 2,
        scratch_shapes=[
            pltpu.VMEM((TOK, CH), f32),
            pltpu.VMEM((WIDTH, CH), f32),
            pltpu.VMEM((LB, 32, 128), f32),
            pltpu.VMEM((LB, 32, 128), f32),
            pltpu.VMEM((2, CH), f32),
        ],
    )(lengths, core.reshape(1), ln_gain, ln_bias, kernel, target, by_y, other_weight, npad, slope)
    hat, sums = kernel_call(
        input_kernel, 8,
        out_shape=(shape(TOK, CH), shape(2, TOK)),
        in_specs=[SMEM] + [VMEM] * 6,
        out_specs=[VMEM] * 2,
        scratch_shapes=[
            pltpu.VMEM((UTT, FR, 128), f32),
            pltpu.VMEM((UTT, FR, 128), f32),
            pltpu.VMEM((1, CH), f32),
        ],
    )(lengths, frames_in, mean, rstd, ln_gain, kernel, gpad)
    sums = lax.psum(sums, "x")
    frames_grad = kernel_call(
        finish_kernel, 5,
        out_shape=shape(TOK, CH, dtype=bf16),
        in_specs=[SMEM, SMEM, SMEM] + [VMEM] * 6,
        out_specs=VMEM,
    )(lengths, place, (TOK * 2 * ny * nz * inverse).reshape(1),
      frames_in, mean, rstd, hat, sums, target)

    small = lax.all_to_all(small.reshape(pieces, 16, 128), ("y", "core"), 0, 0)
    both = kernel_call(
        mix_kernel, 2, out_shape=shape(nz, out_rows * LB + 20, 128), in_specs=[VMEM], out_specs=VMEM
    )(term)
    both = kernel_call(
        fill_kernel, 1,
        out_shape=shape(nz, out_rows * LB + 20, 128),
        in_specs=[VMEM, ANY], out_specs=ANY,
        scratch_shapes=[pltpu.VMEM((16, 128), f32), pltpu.SemaphoreType.DMA((nz,))],
        input_output_aliases={1: 0},
    )(small, both)
    both = lax.all_to_all(both, "z", 0, 0)
    weight_grad, small = kernel_call(
        unmix_kernel, 1,
        out_shape=(shape(out_rows, CH), shape(pieces, 16, 128)),
        in_specs=[SMEM, VMEM], out_specs=[VMEM] * 2,
    )(inverse.reshape(1), both)
    small = lax.all_to_all(small, ("y", "core"), 0, 0)
    tap_grad, gain_grad, bias_grad = kernel_call(
        emit_kernel, 1,
        out_shape=(shape(TAPS, CH), shape(CH), shape(CH)),
        in_specs=[VMEM], out_specs=[VMEM] * 3,
    )(small.reshape(pieces * 16, 128))
    return frames_grad, weight_grad, tap_grad, gain_grad, bias_grad


def solution(mesh):
    nz, ny = 16, 4
    fine = Mesh(mesh.devices.reshape(nz, ny, 2, 4), ("z", "y", "core", "x"))
    dp = ("z", "y", "core")
    return jax.shard_map(
        functools.partial(program, nz=nz, ny=ny),
        mesh=fine,
        in_specs=(P(dp, "x"), P(dp), P("x"), P("x"), P(None, "x"), P(dp, "x"), P(dp, None)),
        out_specs=(P(dp, "x"), P(dp, "x"), P(None, "x"), P("x"), P("x")),
        check_vma=False,
    )
```

```python
import functools

import jax
import jax.numpy as jnp
from jax import lax
from jax.experimental import pallas as pl
from jax.experimental.pallas import tpu as pltpu
from jax.sharding import Mesh, PartitionSpec as P

epsilon = 1e-05
UTT = 4
FR = 256
TOK = UTT * FR
CH = 384
LB = CH // 128
TAPS = 31
HALF = 15
WIDTH = 1536
PADDED = FR + 32
ROWS = 32
f32 = jnp.float32
bf16 = jnp.bfloat16

VMEM = pl.BlockSpec(memory_space=pltpu.VMEM)
ANY = pl.BlockSpec(memory_space=pl.ANY)
SMEM = pl.BlockSpec(memory_space=pltpu.SMEM)


def rows_of(column):
    return jnp.sum(column.T, axis=0, keepdims=True)


def columns_of(row):
    return jnp.broadcast_to(row, (128, FR)).T


def open_kernel(len_ref, weight_ref, x_ref, spread_ref, stat_ref):
    share = weight_ref.shape[0]
    lane = lax.broadcasted_iota(jnp.int32, (16 - share, CH), 1)
    extra = jnp.zeros((16 - share, CH), f32)
    for u in range(UTT):
        extra = jnp.where(lane == u, len_ref[u].astype(f32), extra)
    both = jnp.concatenate([weight_ref[...].astype(f32), extra], axis=0).astype(bf16)
    for z in range(spread_ref.shape[0]):
        spread_ref[z] = both
    for u in range(UTT):
        rows = pl.ds(u * FR, FR)
        parts = [x_ref[rows, pl.ds(l * 128, 128)].astype(f32) for l in range(LB)]
        total = rows_of(parts[0] + parts[1] + parts[2])
        mean = columns_of(total * (1.0 / CH))
        parts = [p - mean for p in parts]
        stat_ref[0:1, rows] = total
        stat_ref[1:2, rows] = rows_of(parts[0] * parts[0] + parts[1] * parts[1] + parts[2] * parts[2])


def valid_rows(length):
    return lax.broadcasted_iota(jnp.int32, (FR, 128), 0) < length


def mix_kernel(term_ref, out_ref):
    nz, share = out_ref.shape[0], WIDTH // 128
    for z in range(nz):
        rows = term_ref[0, z * share : (z + 1) * share, :]
        for j in range(1, term_ref.shape[0]):
            rows = rows + term_ref[j, z * share : (z + 1) * share, :]
        out_ref[z, 0:16, :] = jnp.zeros((16, 128), f32)
        for l in range(LB):
            out_ref[z, 16 + l * share : 16 + (l + 1) * share, :] = rows[:, l * 128 : (l + 1) * 128]
        out_ref[z, 16 + LB * share :, :] = jnp.zeros((4, 128), f32)


def fill_kernel(small_ref, both_ref, out_ref, sum_ref, sem_ref):
    small = small_ref[0]
    for j in range(1, small_ref.shape[0]):
        small = small + small_ref[j]
    sum_ref[...] = small
    copies = [
        pltpu.make_async_copy(sum_ref, out_ref.at[z, 0:16, :], sem_ref.at[z]) for z in range(out_ref.shape[0])
    ]
    for copy in copies:
        copy.start()
    for copy in copies:
        copy.wait()


def unmix_kernel(inverse_ref, both_ref, weight_ref, small_ref):
    share = WIDTH // 128
    both = both_ref[0]
    for z in range(1, both_ref.shape[0]):
        both = both + both_ref[z]
    both = both * inverse_ref[0]
    for l in range(LB):
        weight_ref[:, l * 128 : (l + 1) * 128] = both[16 + l * share : 16 + (l + 1) * share]
    for j in range(small_ref.shape[0]):
        small_ref[j] = both[:16]


def emit_kernel(small_ref, tap_ref, gain_ref, bias_ref):
    for l in range(LB):
        lanes = slice(l * 128, (l + 1) * 128)
        tap_ref[:, lanes] = small_ref[l * 40 : l * 40 + TAPS, :]
        gain_ref[lanes] = small_ref[l * 40 + TAPS, :]
        bias_ref[lanes] = small_ref[l * 40 + TAPS + 1, :]


def forward_kernel(len_ref, core_ref, x_ref, stat_ref, gain_ref, bias_ref, tap_ref, tgt_ref,
                   keep_ref, send_ref, npad_ref, slope_ref, rstd_ref, act_ref, term_ref, mpad_ref, par_ref, mean_ref, *, nz, ny):
    zero16 = jnp.zeros((16, 128), f32)
    par_ref[0:1, :] = gain_ref[...].reshape(1, CH)
    par_ref[1:2, :] = bias_ref[...].reshape(1, CH)
    mpad_ref[0:16, :] = zero16
    mpad_ref[16 + FR : PADDED, :] = zero16
    for u in range(UTT):
        rows = pl.ds(u * FR, FR)
        sums = [stat_ref[j, 0:1, rows] for j in range(4)]
        squares = [stat_ref[j, 1:2, rows] for j in range(4)]
        mean = (sums[0] + sums[1] + sums[2] + sums[3]) * (1.0 / WIDTH)
        spread = squares[0] + squares[1] + squares[2] + squares[3]
        for s in sums:
            gap = s * (1.0 / CH) - mean
            spread = spread + CH * (gap * gap)
        rstd = lax.rsqrt(spread * (1.0 / WIDTH) + epsilon)
        mean_ref[u] = columns_of(mean)
        rstd_ref[u] = columns_of(rstd)

    def step(i, carry):
        u, l = i // LB, i % LB
        rows = pl.ds(pl.multiple_of(u * FR, FR), FR)
        lanes = pl.ds(pl.multiple_of(l * 128, 128), 128)
        keep = valid_rows(len_ref[u])
        normed = (x_ref[rows, lanes].astype(f32) - mean_ref[u]) * rstd_ref[u]
        mpad_ref[16 : 16 + FR, :] = jnp.where(keep, normed * par_ref[0:1, lanes] + par_ref[1:2, lanes], 0.0)
        npad_ref[i, 0:16, :] = zero16
        npad_ref[i, 16 : 16 + FR, :] = jnp.where(keep, normed, 0.0)
        npad_ref[i, 16 + FR : PADDED, :] = zero16
        for r in range(0, FR, ROWS):
            acc = jnp.zeros((ROWS, 128), f32)
            for k in range(TAPS):
                acc = acc + tap_ref[k : k + 1, lanes] * mpad_ref[r + k + 1 : r + k + 1 + ROWS, :]
            gate = jax.nn.sigmoid(acc)
            slope_ref[i, r : r + ROWS, :] = gate * (1.0 + acc * (1.0 - gate))
            here = lax.broadcasted_iota(jnp.int32, (ROWS, 128), 0) + r < len_ref[u]
            act_ref[pl.ds(pl.multiple_of(u * FR + r, ROWS), ROWS), lanes] = jnp.where(
                here, acc * gate, 0.0
            ).astype(bf16)
        return carry

    lax.fori_loop(0, UTT * LB, step, 0)
    term_ref[...] = lax.dot_general(
        tgt_ref[...], act_ref[...], (((0,), (0,)), ((), ())), preferred_element_type=f32
    )
    is_first = core_ref[0] == 0
    share = WIDTH // (2 * nz * ny)
    for z in range(nz):
        for y in range(ny):
            source, goal = (z * ny + y) * 2 * share, (y * nz + z) * share
            first = term_ref[source : source + share, :]
            second = term_ref[source + share : source + 2 * share, :]
            keep_ref[goal : goal + share, :] = jnp.where(is_first, first, second)
            send_ref[goal : goal + share, :] = jnp.where(is_first, second, first)


def backward_kernel(len_ref, core_ref, gain_ref, bias_ref, tap_ref, tgt_ref, own_ref, other_ref, npad_ref, slope_ref,
                    gpad_ref, small_ref, agrad_ref, pw_ref, q_ref, sum_ref, tap_sum_ref, par_ref, *, nz, ny):
    is_first = core_ref[0] == 0
    share = WIDTH // (2 * nz * ny)
    for y in range(ny):
        for z in range(nz):
            mine, its = own_ref[y, z].astype(f32)[:share], other_ref[y, z].astype(f32)[:share]
            goal = (z * ny + y) * 2 * share
            pw_ref[goal : goal + share, :] = jnp.where(is_first, mine, its)
            pw_ref[goal + share : goal + 2 * share, :] = jnp.where(is_first, its, mine)
    agrad_ref[...] = jnp.dot(tgt_ref[...], pw_ref[...].astype(bf16), preferred_element_type=f32)
    par_ref[0:1, :] = gain_ref[...].reshape(1, CH)
    par_ref[1:2, :] = bias_ref[...].reshape(1, CH)
    zero16 = jnp.zeros((16, 128), f32)
    q_ref[...] = jnp.zeros(q_ref.shape, f32)
    sum_ref[...] = jnp.zeros(sum_ref.shape, f32)

    def step(i, carry):
        u, l = i // LB, i % LB
        rows = pl.ds(pl.multiple_of(u * FR, FR), FR)
        lanes = pl.ds(pl.multiple_of(l * 128, 128), 128)
        keep = valid_rows(len_ref[u])
        gpad_ref[i, 0:16, :] = zero16
        gpad_ref[i, 16 + FR : PADDED, :] = zero16
        gpad_ref[i, 16 : 16 + FR, :] = jnp.where(keep, agrad_ref[rows, lanes] * slope_ref[i], 0.0)
        taps = [q_ref[l, k] for k in range(TAPS)]
        total = sum_ref[l, 0:8, :]
        for r in range(0, FR, 8):
            grad = gpad_ref[i, 16 + r : 24 + r, :]
            total = total + grad
            taps = [acc + grad * npad_ref[i, r + k + 1 : r + k + 9, :] for k, acc in enumerate(taps)]
        for k, acc in enumerate(taps):
            q_ref[l, k] = acc
        sum_ref[l, 0:8, :] = total
        sum_ref[l, 8:24, :] += gpad_ref[i, 16:32, :]
        sum_ref[l, 24:40, :] += gpad_ref[i, pl.ds(len_ref[u], 16), :]
        return carry

    lax.fori_loop(0, UTT * LB, step, 0)
    small_ref[...] = jnp.zeros(small_ref.shape, f32)
    row = lax.broadcasted_iota(jnp.int32, (16, 128), 0)
    for l in range(LB):
        lanes = slice(l * 128, (l + 1) * 128)
        for k in range(TAPS):
            tap_sum_ref[0, k : k + 1, :] = jnp.sum(q_ref[l, k], axis=0, keepdims=True)
        total = jnp.sum(sum_ref[l, 0:8, :], axis=0, keepdims=True)
        head, tail = sum_ref[l, 8:24, :], sum_ref[l, 24:40, :]
        tap_sum_ref[1, HALF : HALF + 1, :] = total
        for j in range(1, HALF + 1):
            first = jnp.sum(jnp.where(row < j, head, 0.0), axis=0, keepdims=True)
            last = jnp.sum(jnp.where(row >= 16 - j, tail, 0.0), axis=0, keepdims=True)
            tap_sum_ref[1, HALF - j : HALF - j + 1, :] = total - first
            tap_sum_ref[1, HALF + j : HALF + j + 1, :] = total - last
        q, s, w = tap_sum_ref[0, :TAPS, :], tap_sum_ref[1, :TAPS, :], tap_ref[:, lanes]
        small_ref[l * 40 : l * 40 + TAPS, :] = par_ref[0:1, lanes] * q + par_ref[1:2, lanes] * s
        small_ref[l * 40 + TAPS : l * 40 + TAPS + 1, :] = jnp.sum(w * q, axis=0, keepdims=True)
        small_ref[l * 40 + TAPS + 1 : l * 40 + TAPS + 2, :] = jnp.sum(w * s, axis=0, keepdims=True)


def input_kernel(len_ref, npad_ref, gain_ref, tap_ref, gpad_ref,
                 mgrad_ref, sums_ref, hat_ref, dot_ref, par_ref):
    par_ref[...] = gain_ref[...].reshape(1, CH)

    def step(i, carry):
        u, l = i // LB, i % LB
        lanes = pl.ds(pl.multiple_of(l * 128, 128), 128)
        first = l == 0
        for r in range(0, FR, ROWS):
            acc = jnp.zeros((ROWS, 128), f32)
            for k in range(TAPS):
                acc = acc + tap_ref[k : k + 1, lanes] * gpad_ref[i, r + 31 - k : r + 31 - k + ROWS, :]
            here = lax.broadcasted_iota(jnp.int32, (ROWS, 128), 0) + r < len_ref[u]
            hat = jnp.where(here, acc, 0.0) * par_ref[:, lanes]
            part = pl.ds(pl.multiple_of(u * FR + r, ROWS), ROWS)
            normed = npad_ref[i, 16 + r : 16 + r + ROWS, :]
            mgrad_ref[part, lanes] = hat
            hat_ref[u, r : r + ROWS, :] = jnp.where(first, 0.0, hat_ref[u, r : r + ROWS, :]) + hat
            dot_ref[u, r : r + ROWS, :] = jnp.where(first, 0.0, dot_ref[u, r : r + ROWS, :]) + hat * normed
        return carry

    lax.fori_loop(0, UTT * LB, step, 0)
    for u in range(UTT):
        rows = pl.ds(u * FR, FR)
        sums_ref[0:1, rows] = rows_of(hat_ref[u])
        sums_ref[1:2, rows] = rows_of(dot_ref[u])


def finish_kernel(len_ref, own_ref, scale_ref, npad_ref, rstd_ref, hat_ref, sums_ref, tgt_ref, out_ref):
    scale = scale_ref[0]
    for u in range(UTT):
        rows = pl.ds(u * FR, FR)
        keep = valid_rows(len_ref[u])
        total, dot = columns_of(sums_ref[0:1, rows] * (1.0 / WIDTH)), columns_of(sums_ref[1:2, rows] * (1.0 / WIDTH))
        for l in range(LB):
            lanes = pl.ds(l * 128, 128)
            normed = npad_ref[u * LB + l, 16 : 16 + FR, :]
            grad = rstd_ref[u] * (hat_ref[rows, lanes] - total - normed * dot)
            own = tgt_ref[rows, pl.ds(pl.multiple_of(own_ref[0] * CH + l * 128, 128), 128)].astype(f32)
            out_ref[rows, lanes] = ((jnp.where(keep, own, 0.0) + grad) * scale).astype(bf16)


def kernel_call(kernel, micros, **options):
    return pl.pallas_call(
        kernel, cost_estimate=pl.CostEstimate(flops=0, transcendentals=0, bytes_accessed=micros * 3_000_000), **options
    )


def shape(*dims, dtype=f32):
    return jax.ShapeDtypeStruct(dims, dtype)


def swap(value):
    return lax.ppermute(value, "core", [(0, 1), (1, 0)])


def everyone(value, axis, count):
    return lax.all_to_all(jnp.broadcast_to(value, (count, *value.shape)), axis, 0, 0)


def program(frames_in, lengths, ln_gain, ln_bias, kernel, point_weight, target, *, nz, ny):
    core = lax.axis_index("core")
    place = lax.axis_index("x").reshape(1)
    out_rows = point_weight.shape[0]
    own, stats = kernel_call(
        open_kernel, 3,
        out_shape=(shape(nz, 16, CH, dtype=bf16), shape(2, TOK)),
        in_specs=[SMEM, VMEM, VMEM], out_specs=[VMEM] * 2,
    )(lengths, point_weight, frames_in)
    by_z = lax.all_to_all(own, "z", 0, 0)
    by_y = everyone(by_z, "y", ny)
    other_weight = swap(by_y)
    frame_total = jnp.sum(by_y[:, :, out_rows, :UTT].astype(f32) + other_weight[:, :, out_rows, :UTT].astype(f32))
    inverse = 1.0 / frame_total

    stats = lax.all_gather(stats, "x", axis=0)
    half_rows = WIDTH // 2
    pieces = 2 * ny
    keep, send, npad, slope, rstd = kernel_call(
        functools.partial(forward_kernel, nz=nz, ny=ny), 10,
        out_shape=(
            shape(half_rows, CH),
            shape(half_rows, CH),
            shape(UTT * LB, PADDED, 128),
            shape(UTT * LB, FR, 128),
            shape(UTT, FR, 128),
        ),
        in_specs=[SMEM, SMEM] + [VMEM] * 6,
        out_specs=[VMEM] * 5,
        scratch_shapes=[
            pltpu.VMEM((TOK, CH), bf16),
            pltpu.VMEM((WIDTH, CH), f32),
            pltpu.VMEM((PADDED, 128), f32),
            pltpu.VMEM((2, CH), f32),
            pltpu.VMEM((UTT, FR, 128), f32),
        ],
    )(lengths, core.reshape(1), frames_in, stats, ln_gain, ln_bias, kernel, target)

    other = swap(send)
    term = (keep + other).reshape(ny, nz * out_rows, CH)
    term = lax.all_to_all(term, "y", 0, 0)
    gpad, small = kernel_call(
        functools.partial(backward_kernel, nz=nz, ny=ny), 10,
        out_shape=(shape(UTT * LB, PADDED, 128), shape(pieces * 16, 128)),
        in_specs=[SMEM, SMEM] + [VMEM] * 8,
        out_specs=[VMEM] * 2,
        scratch_shapes=[
            pltpu.VMEM((TOK, CH), f32),
            pltpu.VMEM((WIDTH, CH), f32),
            pltpu.VMEM((LB, 32, 8, 128), f32),
            pltpu.VMEM((LB, 40, 128), f32),
            pltpu.VMEM((2, 32, 128), f32),
            pltpu.VMEM((2, CH), f32),
        ],
    )(lengths, core.reshape(1), ln_gain, ln_bias, kernel, target, by_y, other_weight, npad, slope)
    hat, sums = kernel_call(
        input_kernel, 8,
        out_shape=(shape(TOK, CH), shape(2, TOK)),
        in_specs=[SMEM] + [VMEM] * 4,
        out_specs=[VMEM] * 2,
        scratch_shapes=[
            pltpu.VMEM((UTT, FR, 128), f32),
            pltpu.VMEM((UTT, FR, 128), f32),
            pltpu.VMEM((1, CH), f32),
        ],
    )(lengths, npad, ln_gain, kernel, gpad)
    sums = lax.psum(sums, "x")
    frames_grad = kernel_call(
        finish_kernel, 5,
        out_shape=shape(TOK, CH, dtype=bf16),
        in_specs=[SMEM, SMEM, SMEM] + [VMEM] * 5,
        out_specs=VMEM,
    )(lengths, place, (TOK * 2 * ny * nz * inverse).reshape(1),
      npad, rstd, hat, sums, target)

    small = lax.all_to_all(small.reshape(pieces, 16, 128), ("y", "core"), 0, 0)
    both = kernel_call(
        mix_kernel, 2, out_shape=shape(nz, out_rows * LB + 20, 128), in_specs=[VMEM], out_specs=VMEM
    )(term)
    both = kernel_call(
        fill_kernel, 1,
        out_shape=shape(nz, out_rows * LB + 20, 128),
        in_specs=[VMEM, ANY], out_specs=ANY,
        scratch_shapes=[pltpu.VMEM((16, 128), f32), pltpu.SemaphoreType.DMA((nz,))],
        input_output_aliases={1: 0},
    )(small, both)
    both = lax.all_to_all(both, "z", 0, 0)
    weight_grad, small = kernel_call(
        unmix_kernel, 1,
        out_shape=(shape(out_rows, CH), shape(pieces, 16, 128)),
        in_specs=[SMEM, VMEM], out_specs=[VMEM] * 2,
    )(inverse.reshape(1), both)
    small = lax.all_to_all(small, ("y", "core"), 0, 0)
    tap_grad, gain_grad, bias_grad = kernel_call(
        emit_kernel, 1,
        out_shape=(shape(TAPS, CH), shape(CH), shape(CH)),
        in_specs=[VMEM], out_specs=[VMEM] * 3,
    )(small.reshape(pieces * 16, 128))
    return frames_grad, weight_grad, tap_grad, gain_grad, bias_grad


def solution(mesh):
    nz, ny = 16, 4
    fine = Mesh(mesh.devices.reshape(nz, ny, 2, 4), ("z", "y", "core", "x"))
    dp = ("z", "y", "core")
    return jax.shard_map(
        functools.partial(program, nz=nz, ny=ny),
        mesh=fine,
        in_specs=(P(dp, "x"), P(dp), P("x"), P("x"), P(None, "x"), P(dp, "x"), P(dp, None)),
        out_specs=(P(dp, "x"), P(dp, "x"), P(None, "x"), P("x"), P("x")),
        check_vma=False,
    )
```

```python
import functools

import jax
import jax.numpy as jnp
from jax import lax
from jax.experimental import pallas as pl
from jax.experimental.pallas import tpu as pltpu
from jax.sharding import Mesh, PartitionSpec as P

epsilon = 1e-05
UTT = 4
FR = 256
TOK = UTT * FR
CH = 384
LB = CH // 128
TAPS = 31
HALF = 15
WIDTH = 1536
PADDED = FR + 32
ROWS = 32
f32 = jnp.float32
bf16 = jnp.bfloat16

VMEM = pl.BlockSpec(memory_space=pltpu.VMEM)
SMEM = pl.BlockSpec(memory_space=pltpu.SMEM)


def rows_of(column):
    return jnp.sum(column.T, axis=0, keepdims=True)


def columns_of(row):
    return jnp.broadcast_to(row, (128, FR)).T


def spread_kernel(len_ref, weight_ref, spread_ref):
    share = weight_ref.shape[0]
    lane = lax.broadcasted_iota(jnp.int32, (16 - share, CH), 1)
    extra = jnp.zeros((16 - share, CH), f32)
    for u in range(UTT):
        extra = jnp.where(lane == u, len_ref[u].astype(f32), extra)
    both = jnp.concatenate([weight_ref[...].astype(f32), extra], axis=0).astype(bf16)
    for z in range(spread_ref.shape[0]):
        spread_ref[z] = both


def stats_kernel(x_ref, stat_ref):
    for u in range(UTT):
        rows = pl.ds(u * FR, FR)
        parts = [x_ref[rows, pl.ds(l * 128, 128)].astype(f32) for l in range(LB)]
        total = rows_of(parts[0] + parts[1] + parts[2])
        mean = columns_of(total * (1.0 / CH))
        parts = [p - mean for p in parts]
        stat_ref[0:1, rows] = total
        stat_ref[1:2, rows] = rows_of(parts[0] * parts[0] + parts[1] * parts[1] + parts[2] * parts[2])


def valid_rows(length):
    return lax.broadcasted_iota(jnp.int32, (FR, 128), 0) < length


def mix_kernel(term_ref, small_ref, out_ref):
    nz, share = out_ref.shape[0], WIDTH // 128
    small = small_ref[0]
    for j in range(1, small_ref.shape[0]):
        small = small + small_ref[j]
    for z in range(nz):
        rows = term_ref[0, z * share : (z + 1) * share, :]
        for j in range(1, term_ref.shape[0]):
            rows = rows + term_ref[j, z * share : (z + 1) * share, :]
        for l in range(LB):
            out_ref[z, l * share : (l + 1) * share, :] = rows[:, l * 128 : (l + 1) * 128]
        out_ref[z, LB * share :, :] = small


def unmix_kernel(inverse_ref, both_ref, weight_ref, small_ref):
    share = WIDTH // 128
    both = both_ref[0]
    for z in range(1, both_ref.shape[0]):
        both = both + both_ref[z]
    both = both * inverse_ref[...]
    for l in range(LB):
        weight_ref[:, l * 128 : (l + 1) * 128] = both[l * share : (l + 1) * share]
    for j in range(small_ref.shape[0]):
        small_ref[j] = both[LB * share :]


def emit_kernel(small_ref, tap_ref, gain_ref, bias_ref, rows_ref):
    count = small_ref.shape[1]
    for j in range(small_ref.shape[0]):
        rows_ref[j * count : (j + 1) * count, :] = small_ref[j]
    for l in range(LB):
        lanes = slice(l * 128, (l + 1) * 128)
        tap_ref[:, lanes] = rows_ref[l * 40 : l * 40 + TAPS, :]
        gain_ref[lanes] = rows_ref[l * 40 + TAPS, :]
        bias_ref[lanes] = rows_ref[l * 40 + TAPS + 1, :]


def forward_kernel(len_ref, core_ref, x_ref, stat_ref, gain_ref, bias_ref, tap_ref, tgt_ref,
                   keep_ref, send_ref, npad_ref, slope_ref, rstd_ref, act_ref, term_ref, mpad_ref, par_ref, mean_ref, *, nz, ny):
    zero16 = jnp.zeros((16, 128), f32)
    par_ref[0:1, :] = gain_ref[...].reshape(1, CH)
    par_ref[1:2, :] = bias_ref[...].reshape(1, CH)
    mpad_ref[0:16, :] = zero16
    mpad_ref[16 + FR : PADDED, :] = zero16
    for u in range(UTT):
        rows = pl.ds(u * FR, FR)
        sums = [stat_ref[j, 0:1, rows] for j in range(4)]
        squares = [stat_ref[j, 1:2, rows] for j in range(4)]
        mean = (sums[0] + sums[1] + sums[2] + sums[3]) * (1.0 / WIDTH)
        spread = squares[0] + squares[1] + squares[2] + squares[3]
        for s in sums:
            gap = s * (1.0 / CH) - mean
            spread = spread + CH * (gap * gap)
        rstd = lax.rsqrt(spread * (1.0 / WIDTH) + epsilon)
        mean_ref[u] = columns_of(mean)
        rstd_ref[u] = columns_of(rstd)

    def step(i, carry):
        u, l = i // LB, i % LB
        rows = pl.ds(pl.multiple_of(u * FR, FR), FR)
        lanes = pl.ds(pl.multiple_of(l * 128, 128), 128)
        keep = valid_rows(len_ref[u])
        normed = (x_ref[rows, lanes].astype(f32) - mean_ref[u]) * rstd_ref[u]
        mpad_ref[16 : 16 + FR, :] = jnp.where(keep, normed * par_ref[0:1, lanes] + par_ref[1:2, lanes], 0.0)
        npad_ref[i, 0:16, :] = zero16
        npad_ref[i, 16 : 16 + FR, :] = jnp.where(keep, normed, 0.0)
        npad_ref[i, 16 + FR : PADDED, :] = zero16
        for r in range(0, FR, ROWS):
            acc = jnp.zeros((ROWS, 128), f32)
            for k in range(TAPS):
                acc = acc + tap_ref[k : k + 1, lanes] * mpad_ref[r + k + 1 : r + k + 1 + ROWS, :]
            gate = jax.nn.sigmoid(acc)
            slope_ref[i, r : r + ROWS, :] = gate * (1.0 + acc * (1.0 - gate))
            here = lax.broadcasted_iota(jnp.int32, (ROWS, 128), 0) + r < len_ref[u]
            act_ref[pl.ds(pl.multiple_of(u * FR + r, ROWS), ROWS), lanes] = jnp.where(
                here, acc * gate, 0.0
            ).astype(bf16)
        return carry

    lax.fori_loop(0, UTT * LB, step, 0)
    term_ref[...] = lax.dot_general(
        tgt_ref[...], act_ref[...], (((0,), (0,)), ((), ())), preferred_element_type=f32
    )
    is_first = core_ref[0] == 0
    share = WIDTH // (2 * nz * ny)
    for z in range(nz):
        for y in range(ny):
            source, goal = (z * ny + y) * 2 * share, (y * nz + z) * share
            first = term_ref[source : source + share, :]
            second = term_ref[source + share : source + 2 * share, :]
            keep_ref[goal : goal + share, :] = jnp.where(is_first, first, second)
            send_ref[goal : goal + share, :] = jnp.where(is_first, second, first)


def backward_kernel(len_ref, core_ref, gain_ref, bias_ref, tap_ref, tgt_ref, own_ref, other_ref, npad_ref, slope_ref,
                    gpad_ref, small_ref, inverse_ref, agrad_ref, pw_ref, q_ref, sum_ref, tap_sum_ref, par_ref, rows_ref, *, nz, ny):
    is_first = core_ref[0] == 0
    share = WIDTH // (2 * nz * ny)
    count = jnp.zeros((1, 128), f32)
    for y in range(ny):
        for z in range(nz):
            mine, its = own_ref[y, z].astype(f32), other_ref[y, z].astype(f32)
            count = count + mine[share : share + 1, :128] + its[share : share + 1, :128]
            mine, its = mine[:share], its[:share]
            goal = (z * ny + y) * 2 * share
            pw_ref[goal : goal + share, :] = jnp.where(is_first, mine, its)
            pw_ref[goal + share : goal + 2 * share, :] = jnp.where(is_first, its, mine)
    inverse_ref[...] = 1.0 / jnp.broadcast_to(jnp.sum(count, axis=1, keepdims=True), (1, 128))
    agrad_ref[...] = jnp.dot(tgt_ref[...], pw_ref[...].astype(bf16), preferred_element_type=f32)
    par_ref[0:1, :] = gain_ref[...].reshape(1, CH)
    par_ref[1:2, :] = bias_ref[...].reshape(1, CH)
    zero16 = jnp.zeros((16, 128), f32)
    q_ref[...] = jnp.zeros(q_ref.shape, f32)
    sum_ref[...] = jnp.zeros(sum_ref.shape, f32)

    def step(i, carry):
        u, l = i // LB, i % LB
        rows = pl.ds(pl.multiple_of(u * FR, FR), FR)
        lanes = pl.ds(pl.multiple_of(l * 128, 128), 128)
        keep = valid_rows(len_ref[u])
        gpad_ref[i, 0:16, :] = zero16
        gpad_ref[i, 16 + FR : PADDED, :] = zero16
        gpad_ref[i, 16 : 16 + FR, :] = jnp.where(keep, agrad_ref[rows, lanes] * slope_ref[i], 0.0)
        taps = [q_ref[l, k] for k in range(TAPS)]
        total = sum_ref[l, 0:8, :]
        for r in range(0, FR, 8):
            grad = gpad_ref[i, 16 + r : 24 + r, :]
            total = total + grad
            taps = [acc + grad * npad_ref[i, r + k + 1 : r + k + 9, :] for k, acc in enumerate(taps)]
        for k, acc in enumerate(taps):
            q_ref[l, k] = acc
        sum_ref[l, 0:8, :] = total
        sum_ref[l, 8:24, :] += gpad_ref[i, 16:32, :]
        sum_ref[l, 24:40, :] += gpad_ref[i, pl.ds(len_ref[u], 16), :]
        return carry

    lax.fori_loop(0, UTT * LB, step, 0)
    rows_ref[...] = jnp.zeros(rows_ref.shape, f32)
    row = lax.broadcasted_iota(jnp.int32, (16, 128), 0)
    for l in range(LB):
        lanes = slice(l * 128, (l + 1) * 128)
        for k in range(TAPS):
            tap_sum_ref[0, k : k + 1, :] = jnp.sum(q_ref[l, k], axis=0, keepdims=True)
        total = jnp.sum(sum_ref[l, 0:8, :], axis=0, keepdims=True)
        head, tail = sum_ref[l, 8:24, :], sum_ref[l, 24:40, :]
        tap_sum_ref[1, HALF : HALF + 1, :] = total
        for j in range(1, HALF + 1):
            first = jnp.sum(jnp.where(row < j, head, 0.0), axis=0, keepdims=True)
            last = jnp.sum(jnp.where(row >= 16 - j, tail, 0.0), axis=0, keepdims=True)
            tap_sum_ref[1, HALF - j : HALF - j + 1, :] = total - first
            tap_sum_ref[1, HALF + j : HALF + j + 1, :] = total - last
        q, s, w = tap_sum_ref[0, :TAPS, :], tap_sum_ref[1, :TAPS, :], tap_ref[:, lanes]
        rows_ref[l * 40 : l * 40 + TAPS, :] = par_ref[0:1, lanes] * q + par_ref[1:2, lanes] * s
        rows_ref[l * 40 + TAPS : l * 40 + TAPS + 1, :] = jnp.sum(w * q, axis=0, keepdims=True)
        rows_ref[l * 40 + TAPS + 1 : l * 40 + TAPS + 2, :] = jnp.sum(w * s, axis=0, keepdims=True)
    size = small_ref.shape[1]
    for j in range(small_ref.shape[0]):
        small_ref[j] = rows_ref[j * size : (j + 1) * size, :]


def input_kernel(len_ref, npad_ref, gain_ref, tap_ref, gpad_ref,
                 mgrad_ref, sums_ref, hat_ref, dot_ref, par_ref):
    par_ref[...] = gain_ref[...].reshape(1, CH)

    def step(i, carry):
        u, l = i // LB, i % LB
        lanes = pl.ds(pl.multiple_of(l * 128, 128), 128)
        first = l == 0
        for r in range(0, FR, ROWS):
            acc = jnp.zeros((ROWS, 128), f32)
            for k in range(TAPS):
                acc = acc + tap_ref[k : k + 1, lanes] * gpad_ref[i, r + 31 - k : r + 31 - k + ROWS, :]
            here = lax.broadcasted_iota(jnp.int32, (ROWS, 128), 0) + r < len_ref[u]
            hat = jnp.where(here, acc, 0.0) * par_ref[:, lanes]
            part = pl.ds(pl.multiple_of(u * FR + r, ROWS), ROWS)
            normed = npad_ref[i, 16 + r : 16 + r + ROWS, :]
            mgrad_ref[part, lanes] = hat
            hat_ref[u, r : r + ROWS, :] = jnp.where(first, 0.0, hat_ref[u, r : r + ROWS, :]) + hat
            dot_ref[u, r : r + ROWS, :] = jnp.where(first, 0.0, dot_ref[u, r : r + ROWS, :]) + hat * normed
        return carry

    lax.fori_loop(0, UTT * LB, step, 0)
    for u in range(UTT):
        rows = pl.ds(u * FR, FR)
        sums_ref[0:1, rows] = rows_of(hat_ref[u])
        sums_ref[1:2, rows] = rows_of(dot_ref[u])


def finish_kernel(len_ref, own_ref, inverse_ref, npad_ref, rstd_ref, hat_ref, sums_ref, tgt_ref, out_ref, *, slots):
    scale = inverse_ref[...] * slots
    for u in range(UTT):
        rows = pl.ds(u * FR, FR)
        keep = valid_rows(len_ref[u])
        total, dot = columns_of(sums_ref[0:1, rows] * (1.0 / WIDTH)), columns_of(sums_ref[1:2, rows] * (1.0 / WIDTH))
        for l in range(LB):
            lanes = pl.ds(l * 128, 128)
            normed = npad_ref[u * LB + l, 16 : 16 + FR, :]
            grad = rstd_ref[u] * (hat_ref[rows, lanes] - total - normed * dot)
            own = tgt_ref[rows, pl.ds(pl.multiple_of(own_ref[0] * CH + l * 128, 128), 128)].astype(f32)
            out_ref[rows, lanes] = ((jnp.where(keep, own, 0.0) + grad) * scale).astype(bf16)


def kernel_call(kernel, micros, **options):
    return pl.pallas_call(
        kernel, cost_estimate=pl.CostEstimate(flops=0, transcendentals=0, bytes_accessed=micros * 3_000_000), **options
    )


def shape(*dims, dtype=f32):
    return jax.ShapeDtypeStruct(dims, dtype)


def swap(value):
    return lax.ppermute(value, "core", [(0, 1), (1, 0)])


def everyone(value, axis, count):
    return lax.all_to_all(jnp.broadcast_to(value, (count, *value.shape)), axis, 0, 0)


def program(frames_in, lengths, ln_gain, ln_bias, kernel, point_weight, target, *, nz, ny):
    core = lax.axis_index("core")
    place = lax.axis_index("x").reshape(1)
    out_rows = point_weight.shape[0]
    own = kernel_call(
        spread_kernel, 1, out_shape=shape(nz, 16, CH, dtype=bf16), in_specs=[SMEM, VMEM], out_specs=VMEM
    )(lengths, point_weight)
    stats = kernel_call(stats_kernel, 3, out_shape=shape(2, TOK), in_specs=[VMEM], out_specs=VMEM)(frames_in)
    by_z = lax.all_to_all(own, "z", 0, 0)
    by_y = everyone(by_z, "y", ny)
    other_weight = swap(by_y)

    stats = lax.all_gather(stats, "x", axis=0)
    half_rows = WIDTH // 2
    pieces, piece = 2 * ny, 128 // (2 * ny)
    keep, send, npad, slope, rstd = kernel_call(
        functools.partial(forward_kernel, nz=nz, ny=ny), 10,
        out_shape=(
            shape(half_rows, CH),
            shape(half_rows, CH),
            shape(UTT * LB, PADDED, 128),
            shape(UTT * LB, FR, 128),
            shape(UTT, FR, 128),
        ),
        in_specs=[SMEM, SMEM] + [VMEM] * 6,
        out_specs=[VMEM] * 5,
        scratch_shapes=[
            pltpu.VMEM((TOK, CH), bf16),
            pltpu.VMEM((WIDTH, CH), f32),
            pltpu.VMEM((PADDED, 128), f32),
            pltpu.VMEM((2, CH), f32),
            pltpu.VMEM((UTT, FR, 128), f32),
        ],
    )(lengths, core.reshape(1), frames_in, stats, ln_gain, ln_bias, kernel, target)

    other = swap(send)
    term = (keep + other).reshape(ny, nz * out_rows, CH)
    term = lax.all_to_all(term, "y", 0, 0)
    gpad, small, inverse = kernel_call(
        functools.partial(backward_kernel, nz=nz, ny=ny), 10,
        out_shape=(shape(UTT * LB, PADDED, 128), shape(pieces, piece, 128), shape(1, 128)),
        in_specs=[SMEM, SMEM] + [VMEM] * 8,
        out_specs=[VMEM] * 3,
        scratch_shapes=[
            pltpu.VMEM((TOK, CH), f32),
            pltpu.VMEM((WIDTH, CH), f32),
            pltpu.VMEM((LB, 32, 8, 128), f32),
            pltpu.VMEM((LB, 40, 128), f32),
            pltpu.VMEM((2, 32, 128), f32),
            pltpu.VMEM((2, CH), f32),
            pltpu.VMEM((128, 128), f32),
        ],
    )(lengths, core.reshape(1), ln_gain, ln_bias, kernel, target, by_y, other_weight, npad, slope)
    hat, sums = kernel_call(
        input_kernel, 8,
        out_shape=(shape(TOK, CH), shape(2, TOK)),
        in_specs=[SMEM] + [VMEM] * 4,
        out_specs=[VMEM] * 2,
        scratch_shapes=[
            pltpu.VMEM((UTT, FR, 128), f32),
            pltpu.VMEM((UTT, FR, 128), f32),
            pltpu.VMEM((1, CH), f32),
        ],
    )(lengths, npad, ln_gain, kernel, gpad)
    sums = lax.psum(sums, "x")
    frames_grad = kernel_call(
        functools.partial(finish_kernel, slots=float(TOK * 2 * ny * nz)), 5,
        out_shape=shape(TOK, CH, dtype=bf16),
        in_specs=[SMEM, SMEM] + [VMEM] * 6,
        out_specs=VMEM,
    )(lengths, place, inverse, npad, rstd, hat, sums, target)

    small = lax.all_to_all(small, ("y", "core"), 0, 0)
    both = kernel_call(
        mix_kernel, 2, out_shape=shape(nz, out_rows * LB + piece, 128), in_specs=[VMEM] * 2, out_specs=VMEM
    )(term, small)
    both = lax.all_to_all(both, "z", 0, 0)
    weight_grad, small = kernel_call(
        unmix_kernel, 1,
        out_shape=(shape(out_rows, CH), shape(pieces, piece, 128)),
        in_specs=[VMEM] * 2, out_specs=[VMEM] * 2,
    )(inverse, both)
    small = lax.all_to_all(small, ("y", "core"), 0, 0)
    tap_grad, gain_grad, bias_grad = kernel_call(
        emit_kernel, 1,
        out_shape=(shape(TAPS, CH), shape(CH), shape(CH)),
        in_specs=[VMEM], out_specs=[VMEM] * 3,
        scratch_shapes=[pltpu.VMEM((128, 128), f32)],
    )(small)
    return frames_grad, weight_grad, tap_grad, gain_grad, bias_grad


def solution(mesh):
    nz, ny = 16, 4
    fine = Mesh(mesh.devices.reshape(nz, ny, 2, 4), ("z", "y", "core", "x"))
    dp = ("z", "y", "core")
    return jax.shard_map(
        functools.partial(program, nz=nz, ny=ny),
        mesh=fine,
        in_specs=(P(dp, "x"), P(dp), P("x"), P("x"), P(None, "x"), P(dp, "x"), P(dp, None)),
        out_specs=(P(dp, "x"), P(dp, "x"), P(None, "x"), P("x"), P("x")),
        check_vma=False,
    )
```
